256 devices in a mesh: slab: 64 (over x, y_hi, z), pencil: 4 (over y_lo, core).
Axes of the slice: x: 4, y: 4 (y_hi: 2, y_lo: 2; y = y_hi * 2 + y_lo), z: 8, core: 2. Of those that a mesh axis runs over, the one named last changes fastest.
Arguments:
- fine_blocks: float32 [4, 65536, 3, 256], P('pencil', 'slab'), may hold values from -6 to 6
- owner_slab: int32 [4, 65536, 1], P('pencil', 'slab'), may hold values from 0 to 63; in each aligned block of 1024 rows (0 to 1023, 1024 to 2047, ..., all dimensions but the last counted through in order) at most 32 rows name the same one
- owner_row: int32 [4, 65536], P('pencil', 'slab'), may hold values from 0 to 2047
- valid_counts: int32 [4, 64], P('pencil', 'slab'), may hold values from 768 to 1024
- coarse_field: float32 [3, 256, 256, 1024], P(None, 'slab', 'pencil'), may hold values from -6 to 6
- active: int32 [256, 256, 1024], P('slab', 'pencil'), may hold values 0 or 1
Outputs:
- cleaned: float32 [3, 256, 256, 1024], P(None, 'slab', 'pencil')
The draws below stay inside these ranges and needn't reach their ends.
Inputs may be any that keep to these rules, and one draw needn't show every extreme that they name: `owner_slab`: among the 1024 blocks of one holder (aligned runs along the second dimension) at most 32 name the same slab, and in some runs a slab is named by exactly 32 of them.
All inputs are finite; a program needn't handle non-finite values. No bound on the sum of `active` on one device may be relied on, other than what follows from the above.
Results may differ from the reference program's by a relative error of at most 0.00005.
Values sent between devices are 32-bit elements; how exact they have to be, the bound alone decides.
No kernel may reach another device: no remote copies, remote signals or barrier semaphores. Data moves between devices by JAX's collectives and lax.ppermute only.
A program may use at most 128 MiB of HBM per device.

```python
import math
import jax
import jax.numpy as jnp
import numpy as np

CZ = 4
CY = 64
NX = 1024
BLK_DEV = 1024
FW = 256
SWEEPS = 3
SLABS = 64
BANDS = 4
NZ = 256
NY = 256
HELD = 65536
ROWS_DEV = 2048
CAP = 32


def with_ends(array, own_key, smallest, largest):
    extent = array.shape
    place = [jax.random.randint(jax.random.fold_in(own_key, axis), (), 0, extent[axis]) for axis in range(len(extent))]
    array = array.at[tuple(place)].set(smallest)
    longest = extent.index(max(extent))
    place[longest] = (place[longest] + 1) % extent[longest]
    return array.at[tuple(place)].set(largest)


def levels(own_key, dims, pieces, smallest, largest):
    gain, own = 1.0, jax.random.fold_in(own_key, 6)
    for dim, parts in pieces:
        heights = jnp.exp(jax.random.uniform(jax.random.fold_in(own, dim), (parts,), jnp.float32, smallest / len(pieces), largest / len(pieces)))
        gain = gain * jnp.repeat(heights, dims[dim] // parts).reshape([-1 if axis == dim else 1 for axis in range(len(dims))])
    return gain


def assign_block(key, own, number, rows, count, top, bound, skew):
    ranking = jax.random.permutation(key, count)
    heavy_load, usual = portions_of(count, rows * top, bound, skew, True), portions_of(count, rows * top, bound, skew, False)
    places = jnp.arange(count)

    def named(sizes, rotation):
        used = int((sizes > 0).sum())
        fixed = max(1, used // 4)
        moved = fixed + (places - fixed + rotation * (used - fixed)) % max(1, count - fixed)
        return jnp.zeros((count,), jnp.int32).at[ranking[jnp.where(places < fixed, places, moved)]].set(jnp.asarray(sizes, jnp.int32))

    sizes = jnp.where(number % 4 == 0, named(heavy_load, number // 4), named(usual, number - number // 4 - 1))
    mixed = jax.random.permutation(jax.random.fold_in(own, 3), count)
    giver, receiver = mixed[0:count // 2 * 2:2], mixed[1:count // 2 * 2:2]
    room = jnp.minimum(sizes[giver] - 1, bound - sizes[receiver]) // 2
    room = jnp.where((giver == ranking[0]) | (receiver == ranking[0]) | (sizes[receiver] == 0), 0, jnp.maximum(room, 0))
    moved = jax.random.randint(jax.random.fold_in(own, 4), (count // 2,), 0, 1 << 20) % (room + 1)
    sizes = sizes.at[giver].add(-moved).at[receiver].add(moved)
    labels = jnp.searchsorted(jnp.cumsum(sizes), jnp.arange(rows * top), side="right").astype(jnp.int32)
    listing = labels.reshape(top, rows).T
    listing = listing[jax.random.permutation(jax.random.fold_in(own, 1), rows)]
    rotation = jax.random.randint(jax.random.fold_in(own, 2), (rows, 1), 0, top)
    return jnp.take_along_axis(listing, (jnp.arange(top)[None, :] + rotation) % top, axis=1)


def portions_of(amount, total, bound, lean, full):
    loads = [(1 << 20) // math.isqrt(rank ** lean) + 1 for rank in range(1, amount + 1)]
    largest = bound if full else min(bound, max(-(-total // amount), total * loads[0] // sum(loads)))
    least = 1 if total - largest >= amount - 1 else 0
    given, spare = [largest] + [least] * (amount - 1), total - largest - least * (amount - 1)
    while spare > 0:
        free = [i for i in range(1, amount) if given[i] < largest] or [i for i in range(1, amount) if given[i] < bound]
        whole, budget = sum([loads[i] for i in free]), spare
        for i in free:
            extra = min(bound - given[i], max(1, budget * loads[i] // whole), spare)
            given[i] = given[i] + extra
            spare = spare - extra
    return np.array(given)


def noise(stream_key, dims, width, bound, cuts=(), held_as=jnp.bfloat16):
    result = jax.random.normal(stream_key, dims, jnp.float32) * width
    if len(cuts) > 0:
        result = levels(stream_key, dims, cuts, -0.22, 0.18) * result
    return jnp.clip(result, min=-bound, max=bound).astype(held_as)


def setup_inputs(seed: int = 0) -> dict:
    key_list = jax.random.split(jax.random.key(seed), 7)
    fine_blocks = noise(key_list[0], (BANDS, HELD, 3, FW), 1.0, 6.0, ((0, 4), (1, 64)), jnp.float32)
    owner_slab_keys = jax.random.split(jax.random.fold_in(key_list[1], 1), BANDS * HELD // BLK_DEV)
    owner_slab_turns = jax.random.permutation(jax.random.fold_in(key_list[1], 3), BANDS * HELD // BLK_DEV)
    owner_slab = jax.vmap(lambda own, number: assign_block(jax.random.fold_in(key_list[1], 2), own, number, BLK_DEV, SLABS, 1, CAP, 2))(owner_slab_keys, owner_slab_turns).reshape((BANDS, HELD, 1))
    owner_row = with_ends(jax.random.randint(key_list[2], (BANDS, HELD), 0, ROWS_DEV), jax.random.fold_in(key_list[2], 1), 0, ROWS_DEV - 1).astype(jnp.int32)
    valid_counts = with_ends(jax.random.randint(key_list[3], (BANDS, SLABS), 3 * BLK_DEV // 4, BLK_DEV + 1), jax.random.fold_in(key_list[3], 1), 3 * BLK_DEV // 4, BLK_DEV).astype(jnp.int32)
    coarse_field = noise(key_list[4], (3, NZ, NY, NX), 1.0, 6.0, ((1, 64), (2, 4)), jnp.float32)
    active = with_ends((jax.random.randint(key_list[5], (NZ, NY, NX), 0, 8) < 7).astype(jnp.int32), jax.random.fold_in(key_list[5], 1), 0, 1)
    return dict(fine_blocks=fine_blocks, owner_slab=owner_slab, owner_row=owner_row, valid_counts=valid_counts, coarse_field=coarse_field, active=active)


def neighbours(potential):
    padded = jnp.pad(potential, 1)
    beside = padded[2:, 1:-1, 1:-1] + padded[:-2, 1:-1, 1:-1]
    beside = beside + padded[1:-1, 2:, 1:-1] + padded[1:-1, :-2, 1:-1]
    beside = beside + padded[1:-1, 1:-1, 2:] + padded[1:-1, 1:-1, :-2]
    return beside


def reference(fine_blocks, owner_slab, owner_row, valid_counts, coarse_field, active):
    columns = []
    for band_index in range(BANDS):
        position = jnp.arange(HELD, dtype=jnp.int32)
        holder = position // BLK_DEV
        usable = (position % BLK_DEV) < valid_counts[band_index][holder]
        weight = usable.astype(jnp.float32)
        blocks = fine_blocks[band_index] * weight[:, None, None]
        coarse = (blocks[..., 0::2] + blocks[..., 1::2]) * 0.5
        target = (owner_slab[band_index, :, 0] * ROWS_DEV + owner_row[band_index]).astype(jnp.int32)
        totals = jnp.zeros((SLABS * ROWS_DEV, 3, 128), jnp.float32).at[target].add(coarse)
        number = jnp.zeros((SLABS * ROWS_DEV,), jnp.float32).at[target].add(weight)
        base = coarse_field[:, :, band_index * CY:(band_index + 1) * CY, :]
        base = base.reshape(3, SLABS, CZ, CY, NX // 128, 128).transpose(1, 2, 3, 4, 0, 5)
        base = base.reshape(SLABS * ROWS_DEV, 3, 128)
        averaged = totals / jnp.maximum(number, 1.0)[:, None, None]
        restricted = jnp.where((number > 0.5)[:, None, None], averaged, base)
        column = restricted.reshape(SLABS, CZ, CY, NX // 128, 3, 128)
        column = column.transpose(4, 0, 1, 2, 3, 5).reshape(3, NZ, CY, NX)
        columns.append(column)
    magnetic = jnp.concatenate(columns, axis=2)
    face_x, face_y, face_z = magnetic[0], magnetic[1], magnetic[2]
    next_x = jnp.pad(face_x[:, :, 1:], ((0, 0), (0, 0), (0, 1)))
    next_y = jnp.pad(face_y[:, 1:, :], ((0, 0), (0, 1), (0, 0)))
    next_z = jnp.pad(face_z[1:, :, :], ((0, 1), (0, 0), (0, 0)))
    divergence = (next_x - face_x) + (next_y - face_y) + (next_z - face_z)
    potential = jnp.zeros_like(divergence)
    for sweep_index in range(SWEEPS):
        potential = (neighbours(potential) - divergence) / 6.0
    grad_x = potential - jnp.pad(potential[:, :, :-1], ((0, 0), (0, 0), (1, 0)))
    grad_y = potential - jnp.pad(potential[:, :-1, :], ((0, 0), (1, 0), (0, 0)))
    grad_z = potential - jnp.pad(potential[:-1, :, :], ((1, 0), (0, 0), (0, 0)))
    inside_mask = active.astype(jnp.float32)
    return jnp.stack([face_x - inside_mask * grad_x, face_y - inside_mask * grad_y, face_z - inside_mask * grad_z])
```

```python
import functools

import jax
import jax.numpy as jnp
from jax import lax
from jax.experimental import pallas as pl
from jax.experimental.pallas import tpu as pltpu
from jax.sharding import PartitionSpec as P

F32, BF16 = jnp.float32, jnp.bfloat16
LANES = 128
SLOTS = 32
TAG_ROW = 3 * SLOTS
BOX_ROWS = TAG_ROW + 8
VMEM_BYTES = 48 << 20


def iota(shape, dim):
    return lax.broadcasted_iota(jnp.int32, shape, dim)


def halves(value):
    high = value.astype(BF16)
    return high, (value - high.astype(F32)).astype(BF16)


def dot(left, right):
    return jnp.dot(left, right, preferred_element_type=F32)


def dot_rows(left, right):
    return lax.dot_general(left, right, (((1,), (1,)), ((), ())), preferred_element_type=F32)


def hot(mask):
    return jnp.where(mask, 1.0, 0.0)


def pack_kernel(info, slab, row, fine, box, coarse, slots, tags):
    count_held = slab.shape[1]
    slab_count = tags.shape[0]
    group = box.shape[0]
    step = pl.program_id(0)

    @pl.when(step == 0)
    def _():
        valid = info[0]
        lane_base = info[1]
        width = 3 * LANES
        chunk = min(256, count_held)
        pick = jnp.where(
            iota((2 * LANES, LANES), 0) // 2 == iota((2 * LANES, LANES), 1), 0.5, 0.0
        ).astype(BF16)
        for part in range(3):
            for start in range(0, count_held, chunk):
                rows = slice(start, start + chunk)
                high, low = halves(fine[part, rows, :])
                mean_high, mean_low = halves(dot(high, pick) + dot(low, pick))
                coarse[rows, part * LANES : (part + 1) * LANES] = mean_high
                coarse[rows, width + part * LANES : width + (part + 1) * LANES] = mean_low
        piece = min(LANES, count_held)
        before = hot(iota((piece, piece), 0) < iota((piece, piece), 1)).astype(BF16)
        ones = jnp.ones((piece, piece), BF16)
        running = jnp.zeros((slab_count, piece), F32)
        table = jnp.zeros((slab_count, LANES), F32)
        for start in range(0, count_held, piece):
            lanes = slice(start, start + piece)
            live = iota((1, piece), 1) + start < valid
            target = jnp.where(live, slab[:, lanes], -1)
            named = hot(iota((slab_count, piece), 0) == target)
            named16 = named.astype(BF16)
            earlier = dot(named16, before) + running
            running = running + dot(named16, ones)
            rank = jnp.sum(named * earlier, axis=0, keepdims=True).astype(jnp.int32)
            slots[:, lanes] = jnp.where(live, target * SLOTS + rank, -1)
            tag = row[:, lanes] + 1
            place = hot(iota((LANES, piece), 0) == rank + lane_base).astype(BF16)
            upper = (named * (tag // 64).astype(F32)).astype(BF16)
            lower = (named * (tag % 64).astype(F32)).astype(BF16)
            table = table + dot_rows(upper, place) * 64.0 + dot_rows(lower, place)
        tags[...] = table

    wanted = iota((group * SLOTS, 1), 0) + step * (group * SLOTS)
    chosen = hot(slots[...] == wanted).astype(BF16)
    both = dot(chosen, coarse[...])
    for part in range(3):
        lanes = slice(part * LANES, (part + 1) * LANES)
        low_lanes = slice((3 + part) * LANES, (4 + part) * LANES)
        rows = (both[:, lanes] + both[:, low_lanes]).reshape(group, SLOTS, LANES)
        box[:, part * SLOTS : (part + 1) * SLOTS, :] = rows
    mine = tags[pl.ds(pl.multiple_of(step * group, group), group), :]
    box[:, TAG_ROW:, :] = jnp.broadcast_to(mine[:, None, :], (group, 8, LANES))


def pack(info, slab, row, fine, slab_count):
    count_held = slab.shape[1]
    group = min(8, slab_count)
    whole = lambda *dims: pl.BlockSpec(dims, lambda i: (0,) * len(dims))
    return pl.pallas_call(
        pack_kernel,
        grid=(slab_count // group,),
        in_specs=[
            pl.BlockSpec(memory_space=pltpu.SMEM),
            whole(1, count_held),
            whole(1, count_held),
            whole(3, count_held, 2 * LANES),
        ],
        out_specs=pl.BlockSpec((group, BOX_ROWS, LANES), lambda i: (i, 0, 0)),
        out_shape=jax.ShapeDtypeStruct((slab_count, BOX_ROWS, LANES), F32),
        scratch_shapes=[
            pltpu.VMEM((count_held, 6 * LANES), BF16),
            pltpu.VMEM((1, count_held), jnp.int32),
            pltpu.VMEM((slab_count, LANES), F32),
        ],
        compiler_params=pltpu.CompilerParams(vmem_limit_bytes=VMEM_BYTES),
        name="pack",
    )(info, slab, row, fine)


def accumulate_kernel(
    box, base, field, partial, low_planes, high_planes, low_rows, high_rows, rows16, tags, above
):
    slab_count = box.shape[0]
    step = pl.program_id(0)
    last = pl.num_programs(0) - 1
    plane = last - step
    depth_y, width_x = base.shape[2], base.shape[3]
    tile_rows = depth_y * (width_x // LANES)
    width = 3 * LANES

    @pl.when(step == 0)
    def _():
        tags[...] = jnp.sum(box[:, TAG_ROW, :].reshape(slab_count // 4, 4, LANES), axis=1)
        chunk = min(8, slab_count)
        for part in range(3):
            for start in range(0, slab_count, chunk):
                value = box[start : start + chunk, part * SLOTS : (part + 1) * SLOTS, :]
                high, low = halves(value.reshape(chunk * SLOTS, LANES))
                rows = slice(start * SLOTS, (start + chunk) * SLOTS)
                rows16[rows, part * LANES : (part + 1) * LANES] = high
                rows16[rows, width + part * LANES : width + (part + 1) * LANES] = low
        above[...] = jnp.zeros_like(above)

    index = iota((tile_rows, 1), 0)
    y = index // 64 * 8 + index % 8
    row_tag = (plane * tile_rows + y * 8 + index // 8 % 8 + 1).astype(F32)
    masks = [hot(tags[g : g + 1, :] == row_tag) for g in range(slab_count // 4)]
    counted = functools.reduce(lambda a, b: a + b, masks).astype(BF16)
    number = dot(counted, jnp.ones((LANES, LANES), BF16))
    chosen = jnp.concatenate([mask.astype(BF16) for mask in masks], axis=1)
    both = dot(chosen, rows16[...])
    some = number > 0.5
    scale = 1.0 / jnp.maximum(number, 1.0)
    for part in range(3):
        totals = both[:, part * LANES : (part + 1) * LANES]
        totals = totals + both[:, (3 + part) * LANES : (4 + part) * LANES]
        averaged = totals * scale
        for y8 in range(depth_y // 8):
            for xb in range(width_x // LANES):
                at = slice(y8 * 64 + xb * 8, y8 * 64 + xb * 8 + 8)
                ys, xs = slice(y8 * 8, y8 * 8 + 8), slice(xb * LANES, (xb + 1) * LANES)
                field[part, 0, ys, xs] = jnp.where(some[at], averaged[at], base[part, 0, ys, xs])

    edge_x = iota((8, width_x), 1) == width_x - 1
    last_y = iota((8, width_x), 0) == 7
    for y8 in range(depth_y // 8):
        ys = slice(y8 * 8, y8 * 8 + 8)
        face_x, face_y, face_z = (field[part, 0, ys, :] for part in range(3))
        next_x = jnp.where(edge_x, 0.0, pltpu.roll(face_x, width_x - 1, 1))
        after = field[1, 0, y8 * 8 + 8 : y8 * 8 + 9, :] if y8 * 8 + 8 < depth_y else 0.0
        next_y = jnp.where(last_y, after, pltpu.roll(face_y, 7, 0))
        value = (next_x - face_x) + (next_y - face_y) + (above[ys, :] - face_z)
        partial[0, ys, :] = value
        above[ys, :] = face_z

        @pl.when(step < last)
        def _():
            low_planes[plane - 1, ys, :] = value

        @pl.when(plane < 2)
        def _():
            high_planes[plane, ys, :] = value

        @pl.when(plane == 0)
        def _():
            high_planes[2, ys, :] = face_z

    low_rows[plane] = partial[0, depth_y - 8 :, :]
    face_row = field[1, 0, 0:1, :]
    high_rows[plane] = jnp.where(iota((8, width_x), 0) == 2, face_row, partial[0, 0:8, :])

    @pl.when(plane == 0)
    def _():
        low_rows[last + 1] = field[2, 0, depth_y - 8 :, :]
        high_rows[last + 1] = field[2, 0, 0:8, :]


def accumulate(box, base):
    slab_count = box.shape[0]
    _, depth_z, depth_y, width_x = base.shape
    top = depth_z - 1
    whole = lambda *dims: pl.BlockSpec(dims, lambda i: (0,) * len(dims))
    planes = pl.BlockSpec((3, 1, depth_y, width_x), lambda i: (0, top - i, 0, 0))
    shape = lambda *dims: jax.ShapeDtypeStruct(dims, F32)
    return pl.pallas_call(
        accumulate_kernel,
        grid=(depth_z,),
        in_specs=[whole(*box.shape), planes],
        out_specs=[
            planes,
            pl.BlockSpec((1, depth_y, width_x), lambda i: (top - i, 0, 0)),
            whole(3, depth_y, width_x),
            whole(3, depth_y, width_x),
            whole(depth_z + 1, 8, width_x),
            whole(depth_z + 1, 8, width_x),
        ],
        out_shape=[
            shape(*base.shape),
            shape(depth_z, depth_y, width_x),
            shape(3, depth_y, width_x),
            shape(3, depth_y, width_x),
            shape(depth_z + 1, 8, width_x),
            shape(depth_z + 1, 8, width_x),
        ],
        scratch_shapes=[
            pltpu.VMEM((slab_count * SLOTS, 6 * LANES), BF16),
            pltpu.VMEM((slab_count // 4, LANES), F32),
            pltpu.VMEM((depth_y, width_x), F32),
        ],
        compiler_params=pltpu.CompilerParams(vmem_limit_bytes=VMEM_BYTES),
        name="accumulate",
    )(box, base)


def corner_kernel(below, above, own, beside, low_corner, high_corner):
    planes, _, width_x = below.shape
    line = iota((8, width_x), 0)
    for z in range(planes):
        value = below[z]
        if z < planes - 1:
            value = value + jnp.where(line == 7, own[z, 2:3, :], 0.0)
        value = jnp.where(line > 4, value, above[z])
        beside[z] = value
        if 1 <= z < planes - 1:
            low_corner[z - 1] = value
        if z < 2:
            high_corner[z] = value
        if z == planes - 1:
            high_corner[2] = value


def corners(below, above, own):
    shape = lambda *dims: jax.ShapeDtypeStruct(dims, F32)
    planes, _, width_x = below.shape
    return pl.pallas_call(
        corner_kernel,
        out_shape=[shape(*below.shape), shape(3, 8, width_x), shape(3, 8, width_x)],
        name="corners",
    )(below, above, own)


def correct_kernel(
    flags, field, partial, below, above, beside, below_beside, above_beside, active, out, first, second, third
):
    depth_z, depth_y, width_x = partial.shape
    planes = depth_z + 5
    tiles = depth_y // 8 + 2
    line = iota((8, width_x), 0)
    column = iota((8, width_x), 1)
    has_low_z, has_high_z, has_low_y, has_high_y = (flags[i] for i in range(4))
    sixth = 1.0 / 6.0

    def z_scale(p):
        return has_low_z if p < 3 else (has_high_z if p >= depth_z + 3 else 1.0)

    def y_scale(t):
        return has_low_y if t == 0 else (has_high_y if t == tiles - 1 else 1.0)

    for p in range(planes):
        z = p - 3
        for t in range(tiles):
            ys = slice(t * 8 - 8, t * 8)
            inner = 0 < t < tiles - 1
            if z < 0:
                value = below[p, ys, :] if inner else below_beside[p]
                edge = below_beside[p, 2:3, :]
                if z == -1:
                    value = value + (field[2, 0, ys, :] if inner else beside[depth_z])
            elif z < depth_z:
                value = partial[z, ys, :] if inner else beside[z]
                edge = beside[z, 2:3, :]
                if z == depth_z - 1:
                    value = value + (above[2, ys, :] if inner else above_beside[2])
            else:
                value = above[z - depth_z, ys, :] if inner else above_beside[z - depth_z]
                edge = above_beside[z - depth_z, 2:3, :]
            if t == tiles - 2:
                value = value + jnp.where(line == 7, edge, 0.0)
            first[p, t * 8 : t * 8 + 8, :] = value * (-sixth * z_scale(p) * y_scale(t))

    def around(source, p, t):
        centre = source[p, t * 8 : t * 8 + 8, :]
        total = source[p - 1, t * 8 : t * 8 + 8, :] + source[p + 1, t * 8 : t * 8 + 8, :]
        lower = source[p, t * 8 - 1 : t * 8, :] if t > 0 else 0.0
        upper = source[p, t * 8 + 8 : t * 8 + 9, :] if t < tiles - 1 else 0.0
        total = total + jnp.where(line == 0, lower, pltpu.roll(centre, 1, 0))
        total = total + jnp.where(line == 7, upper, pltpu.roll(centre, 7, 0))
        total = total + jnp.where(column == 0, 0.0, pltpu.roll(centre, 1, 1))
        return total + jnp.where(column == width_x - 1, 0.0, pltpu.roll(centre, width_x - 1, 1))

    for p in range(1, planes - 1):
        for t in range(tiles):
            value = around(first, p, t) * sixth + first[p, t * 8 : t * 8 + 8, :]
            scaled = not (3 <= p < depth_z + 3 and 0 < t < tiles - 1)
            second[p, t * 8 : t * 8 + 8, :] = value * (z_scale(p) * y_scale(t)) if scaled else value
    for p in range(2, depth_z + 3):
        for t in range(tiles - 1):
            value = around(second, p, t) * sixth + first[p, t * 8 : t * 8 + 8, :]
            scaled = not (3 <= p and 0 < t)
            third[p, t * 8 : t * 8 + 8, :] = value * (z_scale(p) * y_scale(t)) if scaled else value
    for z in range(depth_z):
        p = z + 3
        for t in range(1, tiles - 1):
            ys, rows = slice(t * 8 - 8, t * 8), slice(t * 8, t * 8 + 8)
            mask = active[z, ys, :].astype(F32)
            centre = third[p, rows, :]
            left = jnp.where(column == 0, 0.0, pltpu.roll(centre, 1, 1))
            lower = jnp.where(line == 0, third[p, t * 8 - 1 : t * 8, :], pltpu.roll(centre, 1, 0))
            under = third[p - 1, rows, :]
            for part, other in enumerate((left, lower, under)):
                out[part, z, ys, :] = field[part, z, ys, :] - mask * (centre - other)


def correct(flags, field, partial, below, above, beside, below_beside, above_beside, active):
    depth_z, depth_y, width_x = partial.shape
    extended = pltpu.VMEM((depth_z + 5, depth_y + 16, width_x), F32)
    vmem = pl.BlockSpec(memory_space=pltpu.VMEM)
    return pl.pallas_call(
        correct_kernel,
        in_specs=[pl.BlockSpec(memory_space=pltpu.SMEM)] + [vmem] * 8,
        out_specs=vmem,
        out_shape=jax.ShapeDtypeStruct(field.shape, F32),
        scratch_shapes=[extended] * 3,
        compiler_params=pltpu.CompilerParams(vmem_limit_bytes=VMEM_BYTES),
        name="correct",
    )(flags, field, partial, below, above, beside, below_beside, above_beside, active)


def moved(value, axis, steps):
    count = lax.axis_size(axis)
    pairs = [(i, i + steps) for i in range(count) if 0 <= i + steps < count]
    return lax.ppermute(value, axis, pairs)


def shards(fine_blocks, owner_slab, owner_row, valid_counts, coarse_field, active):
    slab_count, band_count = lax.axis_size("slab"), lax.axis_size("pencil")
    slab_at, band_at = lax.axis_index("slab"), lax.axis_index("pencil")
    count_held = fine_blocks.shape[1]
    info = jnp.stack([valid_counts[0, 0], slab_at % 4 * SLOTS])
    fine = fine_blocks[0].transpose(1, 0, 2)
    out_box = pack(info, owner_slab.reshape(1, count_held), owner_row, fine, slab_count)
    box = lax.all_to_all(out_box, "slab", split_axis=0, concat_axis=0, tiled=True)
    field, partial, low_planes, high_planes, low_rows, high_rows = accumulate(box, coarse_field)
    rows_below = moved(low_rows, "pencil", 1)
    rows_above = moved(high_rows, "pencil", -1)
    below = moved(low_planes, "slab", 1)
    above = moved(high_planes, "slab", -1)
    beside, low_corner, high_corner = corners(rows_below, rows_above, high_rows)
    below_beside = moved(low_corner, "slab", 1)
    above_beside = moved(high_corner, "slab", -1)
    flags = jnp.stack(
        [slab_at > 0, slab_at < slab_count - 1, band_at > 0, band_at < band_count - 1]
    ).astype(F32)
    return correct(flags, field, partial, below, above, beside, below_beside, above_beside, active)


def solution(mesh):
    in_specs = (
        P("pencil", "slab", None, None),
        P("pencil", "slab", None),
        P("pencil", "slab"),
        P("pencil", "slab"),
        P(None, "slab", "pencil", None),
        P("slab", "pencil", None),
    )
    out_specs = P(None, "slab", "pencil", None)
    return jax.shard_map(shards, mesh=mesh, in_specs=in_specs, out_specs=out_specs, check_vma=False)
```

```python
import jax
import jax.numpy as jnp
from jax import lax
from jax.experimental import pallas as pl
from jax.experimental.pallas import tpu as pltpu
from jax.sharding import PartitionSpec as P

F32, BF16 = jnp.float32, jnp.bfloat16
LANES = 128
SLOTS = 32
TAG_ROW = 3 * SLOTS
BOX_ROWS = TAG_ROW + 1
PACK_GROUP = 16
PACK_BYTES = 60 << 20
OUTER_BYTES = 24 << 20
INNER_BYTES = 16 << 20
DIVERGE_BYTES = 16 << 20
CORRECT_BYTES = 24 << 20


def iota(shape, dim):
    return lax.broadcasted_iota(jnp.int32, shape, dim)


def halves(value):
    high = value.astype(BF16)
    return high, (value - high.astype(F32)).astype(BF16)


def dot(left, right):
    return jnp.dot(left, right, preferred_element_type=F32)


def dot_rows(left, right):
    return lax.dot_general(left, right, (((1,), (1,)), ((), ())), preferred_element_type=F32)


def hot(mask):
    return jnp.where(mask, 1.0, 0.0)


def pack_kernel(valid_counts, slab, row, fine, out, coarse, chosen, box, arrived, in_sems, out_sems):
    count_held = slab.shape[1]
    slab_count = chosen.shape[0] // SLOTS
    group = min(PACK_GROUP, slab_count)
    valid = valid_counts[0, 0]
    lane_base = lax.axis_index("slab") % 4 * SLOTS
    loads = [
        pltpu.make_async_copy(fine.at[part], arrived.at[part], in_sems.at[part]) for part in range(3)
    ]
    for load in loads:
        load.start()
    piece = min(LANES, count_held)
    before = hot(iota((piece, piece), 0) < iota((piece, piece), 1)).astype(BF16)
    pieces = range(0, count_held, piece)
    named_all, earlier_all, rank_all, running = [], [], [], jnp.zeros((slab_count, 1), F32)
    for start in pieces:
        live = iota((1, piece), 1) + start < valid
        target = jnp.where(live, slab[:, start : start + piece], -1)
        named = hot(iota((slab_count, piece), 0) == target)
        named_all.append(named)
    for named in named_all:
        earlier_all.append(dot(named.astype(BF16), before) + running)
        running = running + jnp.sum(named, axis=1, keepdims=True)
    table = jnp.zeros((slab_count, LANES), F32)
    for start, named, earlier in zip(pieces, named_all, earlier_all):
        lanes = slice(start, start + piece)
        rank = jnp.sum(named * earlier, axis=0, keepdims=True).astype(jnp.int32)
        rank_all.append(hot(iota((SLOTS, piece), 0) == rank).astype(BF16))
        tag = row[:, lanes] + 1
        place = hot(iota((LANES, piece), 0) == rank + lane_base).astype(BF16)
        upper = (named * (tag // 64).astype(F32)).astype(BF16)
        lower = (named * (tag % 64).astype(F32)).astype(BF16)
        table = table + dot_rows(upper, place) * 64.0 + dot_rows(lower, place)
    rank16 = jnp.concatenate(rank_all, axis=1)
    named16 = jnp.concatenate([named.astype(BF16) for named in named_all], axis=1)
    for g in range(slab_count):
        chosen[g * SLOTS : (g + 1) * SLOTS, :] = rank16 * named16[g : g + 1, :]
        start = g * BOX_ROWS + TAG_ROW
        box[start : start + 1, :] = table[g : g + 1]
    pick = jnp.where(
        iota((2 * LANES, LANES), 0) // 2 == iota((2 * LANES, LANES), 1), 0.5, 0.0
    ).astype(BF16)
    chunk = min(256, count_held)
    stores = []
    for part in range(3):
        loads[part].wait()
        for start in range(0, count_held, chunk):
            rows = slice(start, start + chunk)
            high, low = halves(arrived[part, rows, :])
            mean_high, mean_low = halves(dot(high, pick) + dot(low, pick))
            coarse[part, rows, 0:LANES] = mean_high
            coarse[part, rows, LANES:] = mean_low
        for first in range(0, slab_count, group):
            both = dot(chosen[first * SLOTS : (first + group) * SLOTS, :], coarse[part])
            rows = both[:, :LANES] + both[:, LANES:]
            for g in range(group):
                start = (first + g) * BOX_ROWS + part * SLOTS
                box[start : start + SLOTS, :] = rows[g * SLOTS : (g + 1) * SLOTS]
            if part == 2:
                at = slice(first * BOX_ROWS, (first + group) * BOX_ROWS)
                index = first // group
                store = pltpu.make_async_copy(box.at[at], out.at[at], out_sems.at[index])
                store.start()
                stores.append(store)
    for store in stores:
        store.wait()


def pack(valid_counts, slab, row, fine, slab_count):
    count_held = slab.shape[1]
    vmem = pl.BlockSpec(memory_space=pltpu.VMEM)
    hbm = pl.BlockSpec(memory_space=pltpu.HBM)
    return pl.pallas_call(
        pack_kernel,
        in_specs=[pl.BlockSpec(memory_space=pltpu.SMEM), vmem, vmem, hbm],
        out_specs=hbm,
        out_shape=jax.ShapeDtypeStruct((slab_count * BOX_ROWS, LANES), F32),
        scratch_shapes=[
            pltpu.VMEM((3, count_held, 2 * LANES), BF16),
            pltpu.VMEM((slab_count * SLOTS, count_held), BF16),
            pltpu.VMEM((slab_count * BOX_ROWS, LANES), F32),
            pltpu.VMEM((3, count_held, 2 * LANES), F32),
            pltpu.SemaphoreType.DMA((3,)),
            pltpu.SemaphoreType.DMA((max(1, slab_count // PACK_GROUP),)),
        ],
        compiler_params=pltpu.CompilerParams(vmem_limit_bytes=PACK_BYTES),
        name="pack",
    )(valid_counts, slab, row, fine)


OUTER, INNER = (0, 1, 6, 7), (2, 3, 4, 5)


def rows_of(tiles, tile):
    return slice(tiles.index(tile) * 8, tiles.index(tile) * 8 + 8)


def tile_of(outer, inner, part, z, tile):
    if tile in OUTER:
        return outer[part, z, rows_of(OUTER, tile), :]
    return inner[part, z, rows_of(INNER, tile), :]


def divergence_tile(outer, inner, z, tile):
    depth_z, width_x = outer.shape[1], outer.shape[3]
    face_x, face_y, face_z = (tile_of(outer, inner, part, z, tile) for part in range(3))
    above_z = tile_of(outer, inner, 2, z + 1, tile) if z + 1 < depth_z else 0.0
    next_x = jnp.where(
        iota((8, width_x), 1) == width_x - 1, 0.0, pltpu.roll(face_x, width_x - 1, 1)
    )
    after = tile_of(outer, inner, 1, z, tile + 1)[0:1] if tile < 7 else 0.0
    next_y = jnp.where(iota((8, width_x), 0) == 7, after, pltpu.roll(face_y, 7, 0))
    return (next_x - face_x) + (next_y - face_y) + (above_z - face_z)


def put_plane(low_planes, high_planes, depth_z, z, rows, value):
    if z > depth_z - 4:
        low_planes[z - depth_z + 3, rows, :] = value
    if z < 2:
        high_planes[z, rows, :] = value


def sum_tiles(tiles, rows16, line_hot, tile_hot, number, base, field):
    depth_z, depth_y, width_x = base.shape[1:]
    for low_z in range(0, depth_z, 2):
        pairs = [(z, tile) for z in (low_z, low_z + 1) for tile in tiles]
        line16 = line_hot[...]
        chosen = jnp.concatenate(
            [
                line16 * tile_hot[z * 8 + tile : z * 8 + tile + 1, :]
                for z, tile in pairs
            ],
            axis=0,
        )
        both = dot(chosen, rows16[...])
        for at, (z, tile) in enumerate(pairs):
            found = number[z * 8 + tile]
            scale = 1.0 / jnp.maximum(found, 1.0)
            rows = slice(at * 64, at * 64 + 64)
            from_rows, to_rows = slice(tile * 8, tile * 8 + 8), rows_of(tiles, tile)
            for part in range(3):
                totals = both[rows, part * LANES : (part + 1) * LANES]
                totals = totals + both[rows, (3 + part) * LANES : (4 + part) * LANES]
                averaged = totals * scale
                for xb in range(width_x // LANES):
                    xs, at8 = slice(xb * LANES, (xb + 1) * LANES), slice(xb * 8, xb * 8 + 8)
                    field[part, z, to_rows, xs] = jnp.where(
                        found[at8] > 0.5, averaged[at8], base[part, z, from_rows, xs]
                    )


def outer_kernel(
    box, base, field, low_rows, high_rows, rows16, line_hot, tile_hot, number
):
    slab_count = box.shape[0] // BOX_ROWS
    depth_z = base.shape[1]
    width = 3 * LANES
    tag_rows = [box[i * BOX_ROWS + TAG_ROW : (i + 1) * BOX_ROWS, :] for i in range(slab_count)]
    sums = [sum(tag_rows[i + 1 : i + 4], tag_rows[i]) for i in range(0, slab_count, 4)]
    tags = jnp.concatenate(sums, axis=0).astype(jnp.int32) - 1
    tiles, within = tags >> 6, tags & 63
    order = iota((64, LANES), 0)
    order = order % 8 * 8 + order // 8
    counts = jnp.zeros((64, tile_hot.shape[0]), F32)
    for g in range(slab_count // 4):
        lanes = slice(g * LANES, (g + 1) * LANES)
        line16 = hot(within[g : g + 1, :] == order).astype(BF16)
        tile16 = hot(tiles[g : g + 1, :] == iota((tile_hot.shape[0], LANES), 0)).astype(BF16)
        line_hot[:, lanes] = line16
        tile_hot[:, lanes] = tile16
        counts = counts + dot_rows(line16, tile16)
    for tile in range(tile_hot.shape[0]):
        number[tile] = jnp.broadcast_to(counts[:, tile : tile + 1], (64, LANES))
    for part in range(3):
        for i in range(slab_count):
            start = i * BOX_ROWS + part * SLOTS
            high, low = halves(box[start : start + SLOTS, :])
            rows = slice(i * SLOTS, (i + 1) * SLOTS)
            rows16[rows, part * LANES : (part + 1) * LANES] = high
            rows16[rows, width + part * LANES : width + (part + 1) * LANES] = low
    sum_tiles(OUTER, rows16, line_hot, tile_hot, number, base, field)
    for z in range(depth_z):
        high_rows[3 * z : 3 * z + 2, :] = divergence_tile(field, None, z, 0)[0:2]
        high_rows[3 * z + 2 : 3 * z + 3, :] = tile_of(field, None, 1, z, 0)[0:1]
        low_rows[3 * z : 3 * z + 3, :] = divergence_tile(field, None, z, 7)[5:8]
    end = 3 * depth_z
    low_rows[end : end + 3, :] = tile_of(field, None, 2, 0, 7)[5:8]
    high_rows[end : end + 3, :] = tile_of(field, None, 2, 0, 0)[0:3]


def inner_kernel(rows16, line_hot, tile_hot, number, base, field):
    sum_tiles(INNER, rows16, line_hot, tile_hot, number, base, field)


def vmem_call(kernel, shapes, limit, name):
    vmem = pl.BlockSpec(memory_space=pltpu.VMEM)
    return lambda *operands: pl.pallas_call(
        kernel,
        in_specs=[vmem] * len(operands),
        out_specs=[vmem] * len(shapes),
        out_shape=[jax.ShapeDtypeStruct(dims, dtype) for dims, dtype in shapes],
        compiler_params=pltpu.CompilerParams(vmem_limit_bytes=limit),
        name=name,
    )(*operands)


def sum_outer(box, base):
    slots = box.shape[0] // BOX_ROWS * SLOTS
    _, depth_z, depth_y, width_x = base.shape
    line_count = -(-3 * (depth_z + 1) // 8) * 8
    shapes = [
        ((3, depth_z, 8 * len(OUTER), width_x), F32),
        ((line_count, width_x), F32),
        ((line_count, width_x), F32),
        ((slots, 6 * LANES), BF16),
        ((64, slots), BF16),
        ((depth_z * depth_y // 8, slots), BF16),
        ((depth_z * depth_y // 8, 64, LANES), F32),
    ]
    return vmem_call(outer_kernel, shapes, OUTER_BYTES, "sum_outer")(box, base)


def sum_inner(tables, base):
    _, depth_z, _, width_x = base.shape
    shapes = [((3, depth_z, 8 * len(INNER), width_x), F32)]
    return vmem_call(inner_kernel, shapes, INNER_BYTES, "sum_inner")(*tables, base)[0]


def diverge_kernel(outer, inner, own, below, above, partial, beside, low_planes, high_planes):
    depth_z = outer.shape[1]
    for z in range(depth_z):
        for tile in range(8):
            value = divergence_tile(outer, inner, z, tile)
            if tile == 7:
                face = above[3 * z + 2 : 3 * z + 3, :]
                value = value + jnp.where(iota(value.shape, 0) == 7, face, 0.0)
            rows = slice(tile * 8, tile * 8 + 8)
            partial[z, rows, :] = value
            put_plane(low_planes, high_planes, depth_z, z, rows, value)
            if z == 0:
                high_planes[2, rows, :] = tile_of(outer, inner, 2, 0, tile)
    ext = slice(64, 72)
    for z in range(depth_z + 1):
        beside[z, 0:3, :] = above[3 * z : 3 * z + 3, :]
        beside[z, 3:5, :] = jnp.zeros_like(beside[z, 3:5, :])
        under = below[3 * z : 3 * z + 3, :]
        if z < depth_z:
            face = own[3 * z + 2 : 3 * z + 3, :]
            under = under + jnp.where(iota(under.shape, 0) == 2, face, 0.0)
        beside[z, 5:8, :] = under
        if z < depth_z:
            put_plane(low_planes, high_planes, depth_z, z, ext, beside[z])
        else:
            high_planes[2, ext, :] = beside[z]


def diverge(outer, inner, own, below, above):
    depth_z, width_x = outer.shape[1], outer.shape[3]
    shapes = [((depth_z, 64, width_x), F32), ((depth_z + 1, 8, width_x), F32)]
    shapes += [((3, 72, width_x), F32)] * 2
    return vmem_call(diverge_kernel, shapes, DIVERGE_BYTES, "diverge")(
        outer, inner, own, below, above
    )


def correct_kernel(
    outer, inner, partial, beside, below, above, active,
    out, first, second, third, active_here, out_here, in_sem, out_sems
):
    depth_z, depth_y, width_x = partial.shape
    planes = depth_z + 5
    tiles = depth_y // 8 + 2
    line = iota((8, width_x), 0)
    column = iota((8, width_x), 1)
    slab_at, band_at = lax.axis_index("slab"), lax.axis_index("pencil")
    has_low_z = jnp.where(slab_at > 0, 1.0, 0.0)
    has_high_z = jnp.where(slab_at < lax.axis_size("slab") - 1, 1.0, 0.0)
    has_low_y = jnp.where(band_at > 0, 1.0, 0.0)
    has_high_y = jnp.where(band_at < lax.axis_size("pencil") - 1, 1.0, 0.0)
    load = pltpu.make_async_copy(active, active_here, in_sem)
    load.start()
    sixth = 1.0 / 6.0

    def z_scale(p):
        return has_low_z if p < 3 else (has_high_z if p >= depth_z + 3 else 1.0)

    def y_scale(t):
        return has_low_y if t == 0 else (has_high_y if t == tiles - 1 else 1.0)

    def fill(p):
        z = p - 3
        for t in range(tiles):
            inside = 0 < t < tiles - 1
            rows = slice(t * 8 - 8, t * 8) if inside else slice(depth_y, depth_y + 8)
            if z < 0:
                value = below[p, rows, :]
                if z == -1:
                    value = value + (tile_of(outer, inner, 2, 0, t - 1) if inside else beside[depth_z])
            elif z < depth_z:
                value = partial[z, rows, :] if inside else beside[z]
                if z == depth_z - 1:
                    value = value + above[2, rows, :]
            else:
                value = above[z - depth_z, rows, :]
            first[p, t * 8 : t * 8 + 8, :] = value * (-sixth * z_scale(p) * y_scale(t))

    def around(source, p, t):
        centre = source[p, t * 8 : t * 8 + 8, :]
        total = source[p - 1, t * 8 : t * 8 + 8, :] + source[p + 1, t * 8 : t * 8 + 8, :]
        lower = source[p, t * 8 - 1 : t * 8, :] if t > 0 else 0.0
        upper = source[p, t * 8 + 8 : t * 8 + 9, :] if t < tiles - 1 else 0.0
        total = total + jnp.where(line == 0, lower, pltpu.roll(centre, 1, 0))
        total = total + jnp.where(line == 7, upper, pltpu.roll(centre, 7, 0))
        total = total + jnp.where(column == 0, 0.0, pltpu.roll(centre, 1, 1))
        return total + jnp.where(column == width_x - 1, 0.0, pltpu.roll(centre, width_x - 1, 1))

    def sweep(source, target, p, count):
        for t in range(count):
            value = around(source, p, t) * sixth + first[p, t * 8 : t * 8 + 8, :]
            scaled = not (3 <= p < depth_z + 3 and 0 < t < tiles - 1)
            target[p, t * 8 : t * 8 + 8, :] = value * (z_scale(p) * y_scale(t)) if scaled else value

    def finish(z):
        p = z + 3
        for t in range(1, tiles - 1):
            ys, rows = slice(t * 8 - 8, t * 8), slice(t * 8, t * 8 + 8)
            mask = active_here[z, ys, :].astype(F32)
            centre = third[p, rows, :]
            left = jnp.where(column == 0, 0.0, pltpu.roll(centre, 1, 1))
            lower = jnp.where(line == 0, third[p, t * 8 - 1 : t * 8, :], pltpu.roll(centre, 1, 0))
            under = third[p - 1, rows, :]
            for part, other in enumerate((left, lower, under)):
                face = tile_of(outer, inner, part, z, t - 1)
                out_here[part, z, ys, :] = face - mask * (centre - other)
        store = pltpu.make_async_copy(out_here.at[:, z], out.at[:, z], out_sems.at[z])
        store.start()
        return store

    fill(0)
    fill(1)
    load.wait()
    stores = []
    for p in range(1, planes - 1):
        fill(p + 1)
        sweep(first, second, p, tiles)
        if p > 2:
            sweep(second, third, p - 1, tiles - 1)
        if p > 3:
            stores.append(finish(p - 4))
    for store in stores:
        store.wait()


def correct(outer, inner, partial, beside, below, above, active):
    depth_z, depth_y, width_x = partial.shape
    extended = pltpu.VMEM((depth_z + 5, depth_y + 16, width_x), F32)
    vmem = pl.BlockSpec(memory_space=pltpu.VMEM)
    hbm = pl.BlockSpec(memory_space=pltpu.HBM)
    out_dims = (3, depth_z, depth_y, width_x)
    return pl.pallas_call(
        correct_kernel,
        in_specs=[vmem] * 6 + [hbm],
        out_specs=hbm,
        out_shape=jax.ShapeDtypeStruct(out_dims, F32),
        scratch_shapes=[extended] * 3
        + [
            pltpu.VMEM(active.shape, active.dtype),
            pltpu.VMEM(out_dims, F32),
            pltpu.SemaphoreType.DMA,
            pltpu.SemaphoreType.DMA((depth_z,)),
        ],
        compiler_params=pltpu.CompilerParams(vmem_limit_bytes=CORRECT_BYTES),
        name="correct",
    )(outer, inner, partial, beside, below, above, active)


def moved(value, axis, steps):
    count = lax.axis_size(axis)
    pairs = [(i, i + steps) for i in range(count) if 0 <= i + steps < count]
    return lax.ppermute(value, axis, pairs)


def shards(fine_blocks, owner_slab, owner_row, valid_counts, coarse_field, active):
    slab_count = lax.axis_size("slab")
    count_held = fine_blocks.shape[1]
    fine = fine_blocks[0].transpose(1, 0, 2)
    out_box = pack(valid_counts, owner_slab.reshape(1, count_held), owner_row, fine, slab_count)
    out_box = out_box.reshape(slab_count, BOX_ROWS, 1, LANES)
    box = lax.all_to_all(out_box, "slab", split_axis=0, concat_axis=0, tiled=True)
    box = box.reshape(slab_count * BOX_ROWS, LANES)
    outer, low_rows, high_rows, *tables = sum_outer(box, coarse_field)
    rows_below = moved(low_rows, "pencil", 1)
    rows_above = moved(high_rows, "pencil", -1)
    inner = sum_inner(tables, coarse_field)
    partial, beside, low_planes, high_planes = diverge(
        outer, inner, high_rows, rows_below, rows_above
    )
    below = moved(low_planes, "slab", 1)
    above = moved(high_planes, "slab", -1)
    return correct(outer, inner, partial, beside, below, above, active)


def solution(mesh):
    in_specs = (
        P("pencil", "slab", None, None),
        P("pencil", "slab", None),
        P("pencil", "slab"),
        P("pencil", "slab"),
        P(None, "slab", "pencil", None),
        P("slab", "pencil", None),
    )
    out_specs = P(None, "slab", "pencil", None)
    return jax.shard_map(shards, mesh=mesh, in_specs=in_specs, out_specs=out_specs, check_vma=False)
```

```python
import jax
import jax.numpy as jnp
from jax import lax
from jax.experimental import pallas as pl
from jax.experimental.pallas import tpu as pltpu
from jax.sharding import PartitionSpec as P

F32, BF16 = jnp.float32, jnp.bfloat16
LANES = 128
SLOTS = 32
TAG_ROW = 3 * SLOTS
BOX_ROWS = TAG_ROW + 1
PACK_GROUP = 16
PACK_BYTES = 60 << 20
OUTER_BYTES = 24 << 20
INNER_BYTES = 16 << 20
DIVERGE_BYTES = 16 << 20
CORRECT_BYTES = 24 << 20


def iota(shape, dim):
    return lax.broadcasted_iota(jnp.int32, shape, dim)


def halves(value):
    high = value.astype(BF16)
    return high, (value - high.astype(F32)).astype(BF16)


def dot(left, right):
    return jnp.dot(left, right, preferred_element_type=F32)


def dot_rows(left, right):
    return lax.dot_general(left, right, (((1,), (1,)), ((), ())), preferred_element_type=F32)


def hot(mask):
    return jnp.where(mask, 1.0, 0.0)


def pack_kernel(valid_counts, slab, row, fine, out, coarse, chosen, box, arrived, in_sems, out_sems):
    count_held = slab.shape[1]
    slab_count = chosen.shape[0] // SLOTS
    group = min(PACK_GROUP, slab_count)
    valid = valid_counts[0, 0]
    lane_base = lax.axis_index("slab") % 4 * SLOTS
    loads = [
        pltpu.make_async_copy(fine.at[part], arrived.at[part], in_sems.at[part]) for part in range(3)
    ]
    for load in loads:
        load.start()
    piece = min(LANES, count_held)
    before = hot(iota((piece, piece), 0) < iota((piece, piece), 1)).astype(BF16)
    pieces = range(0, count_held, piece)
    named_all, earlier_all, rank_all, running = [], [], [], jnp.zeros((slab_count, 1), F32)
    for start in pieces:
        live = iota((1, piece), 1) + start < valid
        target = jnp.where(live, slab[:, start : start + piece], -1)
        named = hot(iota((slab_count, piece), 0) == target)
        named_all.append(named)
    for named in named_all:
        earlier_all.append(dot(named.astype(BF16), before) + running)
        running = running + jnp.sum(named, axis=1, keepdims=True)
    table = jnp.zeros((slab_count, LANES), F32)
    for start, named, earlier in zip(pieces, named_all, earlier_all):
        lanes = slice(start, start + piece)
        rank = jnp.sum(named * earlier, axis=0, keepdims=True).astype(jnp.int32)
        rank_all.append(hot(iota((SLOTS, piece), 0) == rank).astype(BF16))
        tag = row[:, lanes] + 1
        place = hot(iota((LANES, piece), 0) == rank + lane_base).astype(BF16)
        upper = (named * (tag // 64).astype(F32)).astype(BF16)
        lower = (named * (tag % 64).astype(F32)).astype(BF16)
        table = table + dot_rows(upper, place) * 64.0 + dot_rows(lower, place)
    rank16 = jnp.concatenate(rank_all, axis=1)
    named16 = jnp.concatenate([named.astype(BF16) for named in named_all], axis=1)
    for g in range(slab_count):
        chosen[g * SLOTS : (g + 1) * SLOTS, :] = rank16 * named16[g : g + 1, :]
        start = g * BOX_ROWS + TAG_ROW
        box[start : start + 1, :] = table[g : g + 1]
    pick = jnp.where(
        iota((2 * LANES, LANES), 0) // 2 == iota((2 * LANES, LANES), 1), 0.5, 0.0
    ).astype(BF16)
    chunk = min(256, count_held)
    stores = []
    for part in range(3):
        loads[part].wait()
        for start in range(0, count_held, chunk):
            rows = slice(start, start + chunk)
            high, low = halves(arrived[part, rows, :])
            mean_high, mean_low = halves(dot(high, pick) + dot(low, pick))
            coarse[part, rows, 0:LANES] = mean_high
            coarse[part, rows, LANES:] = mean_low
        for first in range(0, slab_count, group):
            both = dot(chosen[first * SLOTS : (first + group) * SLOTS, :], coarse[part])
            rows = both[:, :LANES] + both[:, LANES:]
            for g in range(group):
                start = (first + g) * BOX_ROWS + part * SLOTS
                box[start : start + SLOTS, :] = rows[g * SLOTS : (g + 1) * SLOTS]
            if part == 2:
                at = slice(first * BOX_ROWS, (first + group) * BOX_ROWS)
                index = first // group
                store = pltpu.make_async_copy(box.at[at], out.at[at], out_sems.at[index])
                store.start()
                stores.append(store)
    for store in stores:
        store.wait()


def pack(valid_counts, slab, row, fine, slab_count):
    count_held = slab.shape[1]
    vmem = pl.BlockSpec(memory_space=pltpu.VMEM)
    hbm = pl.BlockSpec(memory_space=pltpu.HBM)
    return pl.pallas_call(
        pack_kernel,
        in_specs=[pl.BlockSpec(memory_space=pltpu.SMEM), vmem, vmem, hbm],
        out_specs=hbm,
        out_shape=jax.ShapeDtypeStruct((slab_count * BOX_ROWS, LANES), F32),
        scratch_shapes=[
            pltpu.VMEM((3, count_held, 2 * LANES), BF16),
            pltpu.VMEM((slab_count * SLOTS, count_held), BF16),
            pltpu.VMEM((slab_count * BOX_ROWS, LANES), F32),
            pltpu.VMEM((3, count_held, 2 * LANES), F32),
            pltpu.SemaphoreType.DMA((3,)),
            pltpu.SemaphoreType.DMA((max(1, slab_count // PACK_GROUP),)),
        ],
        compiler_params=pltpu.CompilerParams(vmem_limit_bytes=PACK_BYTES),
        name="pack",
    )(valid_counts, slab, row, fine)


OUTER, INNER = (0, 1, 6, 7), (2, 3, 4, 5)
EARLY, LATE = (0, 6, 7), (1, 2, 3, 4, 5)


def rows_of(tiles, tile):
    return slice(tiles.index(tile) * 8, tiles.index(tile) * 8 + 8)


def tile_of(outer, inner, part, z, tile):
    if tile in OUTER:
        return outer[part, z, rows_of(OUTER, tile), :]
    return inner[part, z, rows_of(INNER, tile), :]


def divergence_tile(outer, inner, z, tile):
    depth_z, width_x = outer.shape[1], outer.shape[3]
    face_x, face_y, face_z = (tile_of(outer, inner, part, z, tile) for part in range(3))
    above_z = tile_of(outer, inner, 2, z + 1, tile) if z + 1 < depth_z else 0.0
    next_x = jnp.where(
        iota((8, width_x), 1) == width_x - 1, 0.0, pltpu.roll(face_x, width_x - 1, 1)
    )
    after = tile_of(outer, inner, 1, z, tile + 1)[0:1] if tile < 7 else 0.0
    next_y = jnp.where(iota((8, width_x), 0) == 7, after, pltpu.roll(face_y, 7, 0))
    return (next_x - face_x) + (next_y - face_y) + (above_z - face_z)


def put_plane(low_planes, high_planes, depth_z, z, rows, value):
    if z > depth_z - 4:
        low_planes[z - depth_z + 3, rows, :] = value
    if z < 2:
        high_planes[z, rows, :] = value


def sum_tiles(tiles, rows16, line_hot, tile_hot, number, base, field):
    depth_z, depth_y, width_x = base.shape[1:]
    for low_z in range(0, depth_z, 2):
        pairs = [(z, tile) for z in (low_z, low_z + 1) for tile in tiles]
        line16 = line_hot[...]
        chosen = jnp.concatenate(
            [
                line16 * tile_hot[z * 8 + tile : z * 8 + tile + 1, :]
                for z, tile in pairs
            ],
            axis=0,
        )
        both = dot(chosen, rows16[...])
        for at, (z, tile) in enumerate(pairs):
            found = number[z * 8 + tile]
            scale = 1.0 / jnp.maximum(found, 1.0)
            rows = slice(at * 64, at * 64 + 64)
            from_rows, to_rows = slice(tile * 8, tile * 8 + 8), rows_of(tiles, tile)
            for part in range(3):
                totals = both[rows, part * LANES : (part + 1) * LANES]
                totals = totals + both[rows, (3 + part) * LANES : (4 + part) * LANES]
                averaged = totals * scale
                for xb in range(width_x // LANES):
                    xs, at8 = slice(xb * LANES, (xb + 1) * LANES), slice(xb * 8, xb * 8 + 8)
                    field[part, z, to_rows, xs] = jnp.where(
                        found[at8] > 0.5, averaged[at8], base[part, z, from_rows, xs]
                    )


def outer_kernel(
    box, base, field, low_rows, high_rows, low_planes, high_planes, rows16, line_hot, tile_hot, number
):
    slab_count = box.shape[0] // BOX_ROWS
    depth_z = base.shape[1]
    width = 3 * LANES
    tag_rows = [box[i * BOX_ROWS + TAG_ROW : (i + 1) * BOX_ROWS, :] for i in range(slab_count)]
    sums = [sum(tag_rows[i + 1 : i + 4], tag_rows[i]) for i in range(0, slab_count, 4)]
    tags = jnp.concatenate(sums, axis=0).astype(jnp.int32) - 1
    tiles, within = tags >> 6, tags & 63
    order = iota((64, LANES), 0)
    order = order % 8 * 8 + order // 8
    counts = jnp.zeros((64, tile_hot.shape[0]), F32)
    for g in range(slab_count // 4):
        lanes = slice(g * LANES, (g + 1) * LANES)
        line16 = hot(within[g : g + 1, :] == order).astype(BF16)
        tile16 = hot(tiles[g : g + 1, :] == iota((tile_hot.shape[0], LANES), 0)).astype(BF16)
        line_hot[:, lanes] = line16
        tile_hot[:, lanes] = tile16
        counts = counts + dot_rows(line16, tile16)
    for tile in range(tile_hot.shape[0]):
        number[tile] = jnp.broadcast_to(counts[:, tile : tile + 1], (64, LANES))
    for part in range(3):
        for i in range(slab_count):
            start = i * BOX_ROWS + part * SLOTS
            high, low = halves(box[start : start + SLOTS, :])
            rows = slice(i * SLOTS, (i + 1) * SLOTS)
            rows16[rows, part * LANES : (part + 1) * LANES] = high
            rows16[rows, width + part * LANES : width + (part + 1) * LANES] = low
    sum_tiles(OUTER, rows16, line_hot, tile_hot, number, base, field)
    for z in range(depth_z):
        for tile in EARLY:
            value = divergence_tile(field, None, z, tile)
            put_plane(low_planes, high_planes, depth_z, z, rows_of(EARLY, tile), value)
            if z == 0:
                high_planes[2, rows_of(EARLY, tile), :] = tile_of(field, None, 2, 0, tile)
            if tile == 0:
                high_rows[3 * z : 3 * z + 2, :] = value[0:2]
                high_rows[3 * z + 2 : 3 * z + 3, :] = tile_of(field, None, 1, z, 0)[0:1]
            if tile == 7:
                low_rows[3 * z : 3 * z + 3, :] = value[5:8]
    end = 3 * depth_z
    low_rows[end : end + 3, :] = tile_of(field, None, 2, 0, 7)[5:8]
    high_rows[end : end + 3, :] = tile_of(field, None, 2, 0, 0)[0:3]


def inner_kernel(rows16, line_hot, tile_hot, number, base, field):
    sum_tiles(INNER, rows16, line_hot, tile_hot, number, base, field)


def vmem_call(kernel, shapes, limit, name):
    vmem = pl.BlockSpec(memory_space=pltpu.VMEM)
    return lambda *operands: pl.pallas_call(
        kernel,
        in_specs=[vmem] * len(operands),
        out_specs=[vmem] * len(shapes),
        out_shape=[jax.ShapeDtypeStruct(dims, dtype) for dims, dtype in shapes],
        compiler_params=pltpu.CompilerParams(vmem_limit_bytes=limit),
        name=name,
    )(*operands)


def sum_outer(box, base):
    slots = box.shape[0] // BOX_ROWS * SLOTS
    _, depth_z, depth_y, width_x = base.shape
    line_count = -(-3 * (depth_z + 1) // 8) * 8
    shapes = [
        ((3, depth_z, 8 * len(OUTER), width_x), F32),
        ((line_count, width_x), F32),
        ((line_count, width_x), F32),
        ((3, 8 * len(EARLY), width_x), F32),
        ((3, 8 * len(EARLY), width_x), F32),
        ((slots, 6 * LANES), BF16),
        ((64, slots), BF16),
        ((depth_z * depth_y // 8, slots), BF16),
        ((depth_z * depth_y // 8, 64, LANES), F32),
    ]
    return vmem_call(outer_kernel, shapes, OUTER_BYTES, "sum_outer")(box, base)


def sum_inner(tables, base):
    _, depth_z, _, width_x = base.shape
    shapes = [((3, depth_z, 8 * len(INNER), width_x), F32)]
    return vmem_call(inner_kernel, shapes, INNER_BYTES, "sum_inner")(*tables, base)[0]


def diverge_kernel(
    outer, inner, own, below, above, below_early, above_early, partial, beside, low_planes, high_planes
):
    del below_early, above_early
    depth_z = outer.shape[1]
    for z in range(depth_z):
        for tile in range(8):
            value = divergence_tile(outer, inner, z, tile)
            if tile == 7:
                face = above[3 * z + 2 : 3 * z + 3, :]
                value = value + jnp.where(iota(value.shape, 0) == 7, face, 0.0)
            partial[z, tile * 8 : tile * 8 + 8, :] = value
            if tile in LATE:
                put_plane(low_planes, high_planes, depth_z, z, rows_of(LATE, tile), value)
                if z == 0:
                    high_planes[2, rows_of(LATE, tile), :] = tile_of(outer, inner, 2, 0, tile)
    ext = slice(8 * len(LATE), 8 * len(LATE) + 8)
    for z in range(depth_z + 1):
        beside[z, 0:3, :] = above[3 * z : 3 * z + 3, :]
        beside[z, 3:5, :] = jnp.zeros_like(beside[z, 3:5, :])
        under = below[3 * z : 3 * z + 3, :]
        if z < depth_z:
            face = own[3 * z + 2 : 3 * z + 3, :]
            under = under + jnp.where(iota(under.shape, 0) == 2, face, 0.0)
        beside[z, 5:8, :] = under
        if z < depth_z:
            put_plane(low_planes, high_planes, depth_z, z, ext, beside[z])
        else:
            high_planes[2, ext, :] = beside[z]


def diverge(outer, inner, own, below, above, early):
    depth_z, width_x = outer.shape[1], outer.shape[3]
    shape = lambda *dims: jax.ShapeDtypeStruct(dims, F32)
    vmem = pl.BlockSpec(memory_space=pltpu.VMEM)
    return pl.pallas_call(
        diverge_kernel,
        in_specs=[vmem] * 5 + [pl.BlockSpec(memory_space=pl.ANY)] * 2,
        out_specs=[vmem] * 4,
        out_shape=[shape(depth_z, 64, width_x), shape(depth_z + 1, 8, width_x)]
        + [shape(3, 8 * len(LATE) + 8, width_x)] * 2,
        compiler_params=pltpu.CompilerParams(vmem_limit_bytes=DIVERGE_BYTES),
        name="diverge",
    )(outer, inner, own, below, above, *early)


def correct_kernel(
    outer, inner, partial, beside, below_early, above_early, below_late, above_late, active,
    out, first, second, third, active_here, out_here, in_sem, out_sems
):
    depth_z, depth_y, width_x = partial.shape
    planes = depth_z + 5
    tiles = depth_y // 8 + 2
    line = iota((8, width_x), 0)
    column = iota((8, width_x), 1)
    slab_at, band_at = lax.axis_index("slab"), lax.axis_index("pencil")
    has_low_z = jnp.where(slab_at > 0, 1.0, 0.0)
    has_high_z = jnp.where(slab_at < lax.axis_size("slab") - 1, 1.0, 0.0)
    has_low_y = jnp.where(band_at > 0, 1.0, 0.0)
    has_high_y = jnp.where(band_at < lax.axis_size("pencil") - 1, 1.0, 0.0)
    load = pltpu.make_async_copy(active, active_here, in_sem)
    load.start()
    sixth = 1.0 / 6.0
    ext = slice(8 * len(LATE), 8 * len(LATE) + 8)

    def z_scale(p):
        return has_low_z if p < 3 else (has_high_z if p >= depth_z + 3 else 1.0)

    def y_scale(t):
        return has_low_y if t == 0 else (has_high_y if t == tiles - 1 else 1.0)

    def arrived(early, late, plane, t, divergence):
        if not 0 < t < tiles - 1:
            return late[plane, ext, :]
        if t - 1 in LATE:
            return late[plane, rows_of(LATE, t - 1), :]
        value = early[plane, rows_of(EARLY, t - 1), :]
        if t - 1 == 7 and divergence:
            face = late[plane, ext.start + 2 : ext.start + 3, :]
            value = value + jnp.where(line == 7, face, 0.0)
        return value

    def fill(p):
        z = p - 3
        for t in range(tiles):
            inside = 0 < t < tiles - 1
            if z < 0:
                value = arrived(below_early, below_late, p, t, True)
                if z == -1:
                    value = value + (tile_of(outer, inner, 2, 0, t - 1) if inside else beside[depth_z])
            elif z < depth_z:
                value = partial[z, t * 8 - 8 : t * 8, :] if inside else beside[z]
                if z == depth_z - 1:
                    value = value + arrived(above_early, above_late, 2, t, False)
            else:
                value = arrived(above_early, above_late, z - depth_z, t, True)
            first[p, t * 8 : t * 8 + 8, :] = value * (-sixth * z_scale(p) * y_scale(t))

    def around(source, p, t):
        centre = source[p, t * 8 : t * 8 + 8, :]
        total = source[p - 1, t * 8 : t * 8 + 8, :] + source[p + 1, t * 8 : t * 8 + 8, :]
        lower = source[p, t * 8 - 1 : t * 8, :] if t > 0 else 0.0
        upper = source[p, t * 8 + 8 : t * 8 + 9, :] if t < tiles - 1 else 0.0
        total = total + jnp.where(line == 0, lower, pltpu.roll(centre, 1, 0))
        total = total + jnp.where(line == 7, upper, pltpu.roll(centre, 7, 0))
        total = total + jnp.where(column == 0, 0.0, pltpu.roll(centre, 1, 1))
        return total + jnp.where(column == width_x - 1, 0.0, pltpu.roll(centre, width_x - 1, 1))

    def sweep(source, target, p, count):
        for t in range(count):
            value = around(source, p, t) * sixth + first[p, t * 8 : t * 8 + 8, :]
            scaled = not (3 <= p < depth_z + 3 and 0 < t < tiles - 1)
            target[p, t * 8 : t * 8 + 8, :] = value * (z_scale(p) * y_scale(t)) if scaled else value

    def finish(z):
        p = z + 3
        for t in range(1, tiles - 1):
            ys, rows = slice(t * 8 - 8, t * 8), slice(t * 8, t * 8 + 8)
            mask = active_here[z, ys, :].astype(F32)
            centre = third[p, rows, :]
            left = jnp.where(column == 0, 0.0, pltpu.roll(centre, 1, 1))
            lower = jnp.where(line == 0, third[p, t * 8 - 1 : t * 8, :], pltpu.roll(centre, 1, 0))
            under = third[p - 1, rows, :]
            for part, other in enumerate((left, lower, under)):
                face = tile_of(outer, inner, part, z, t - 1)
                out_here[part, z, ys, :] = face - mask * (centre - other)
        store = pltpu.make_async_copy(out_here.at[:, z], out.at[:, z], out_sems.at[z])
        store.start()
        return store

    fill(0)
    fill(1)
    load.wait()
    stores = []
    for p in range(1, planes - 1):
        fill(p + 1)
        sweep(first, second, p, tiles)
        if p > 2:
            sweep(second, third, p - 1, tiles - 1)
        if p > 3:
            stores.append(finish(p - 4))
    for store in stores:
        store.wait()


def correct(outer, inner, partial, beside, arrivals, active):
    depth_z, depth_y, width_x = partial.shape
    extended = pltpu.VMEM((depth_z + 5, depth_y + 16, width_x), F32)
    vmem = pl.BlockSpec(memory_space=pltpu.VMEM)
    hbm = pl.BlockSpec(memory_space=pltpu.HBM)
    out_dims = (3, depth_z, depth_y, width_x)
    return pl.pallas_call(
        correct_kernel,
        in_specs=[vmem] * 8 + [hbm],
        out_specs=hbm,
        out_shape=jax.ShapeDtypeStruct(out_dims, F32),
        scratch_shapes=[extended] * 3
        + [
            pltpu.VMEM(active.shape, active.dtype),
            pltpu.VMEM(out_dims, F32),
            pltpu.SemaphoreType.DMA,
            pltpu.SemaphoreType.DMA((depth_z,)),
        ],
        compiler_params=pltpu.CompilerParams(vmem_limit_bytes=CORRECT_BYTES),
        name="correct",
    )(outer, inner, partial, beside, *arrivals, active)


def moved(value, axis, steps):
    count = lax.axis_size(axis)
    pairs = [(i, i + steps) for i in range(count) if 0 <= i + steps < count]
    return lax.ppermute(value, axis, pairs)


def shards(fine_blocks, owner_slab, owner_row, valid_counts, coarse_field, active):
    slab_count = lax.axis_size("slab")
    count_held = fine_blocks.shape[1]
    fine = fine_blocks[0].transpose(1, 0, 2)
    out_box = pack(valid_counts, owner_slab.reshape(1, count_held), owner_row, fine, slab_count)
    out_box = out_box.reshape(slab_count, BOX_ROWS, 1, LANES)
    box = lax.all_to_all(out_box, "slab", split_axis=0, concat_axis=0, tiled=True)
    box = box.reshape(slab_count * BOX_ROWS, LANES)
    outer, low_rows, high_rows, low_early, high_early, *tables = sum_outer(box, coarse_field)
    rows_below = moved(low_rows, "pencil", 1)
    rows_above = moved(high_rows, "pencil", -1)
    below_early = moved(low_early, "slab", 1)
    above_early = moved(high_early, "slab", -1)
    inner = sum_inner(tables, coarse_field)
    early = (below_early, above_early)
    partial, beside, low_late, high_late = diverge(
        outer, inner, high_rows, rows_below, rows_above, early
    )
    below_late = moved(low_late, "slab", 1)
    above_late = moved(high_late, "slab", -1)
    arrivals = (*early, below_late, above_late)
    return correct(outer, inner, partial, beside, arrivals, active)


def solution(mesh):
    in_specs = (
        P("pencil", "slab", None, None),
        P("pencil", "slab", None),
        P("pencil", "slab"),
        P("pencil", "slab"),
        P(None, "slab", "pencil", None),
        P("slab", "pencil", None),
    )
    out_specs = P(None, "slab", "pencil", None)
    return jax.shard_map(shards, mesh=mesh, in_specs=in_specs, out_specs=out_specs, check_vma=False)
```

```python
import jax
import jax.numpy as jnp
from jax import lax
from jax.experimental import pallas as pl
from jax.experimental.pallas import tpu as pltpu
from jax.sharding import PartitionSpec as P

F32, BF16 = jnp.float32, jnp.bfloat16
LANES = 128
SLOTS = 32
TAG_ROW = 3 * SLOTS
BOX_ROWS = TAG_ROW + 1
PACK_GROUP = 16
PACK_BYTES = 60 << 20
OUTER_BYTES = 24 << 20
INNER_BYTES = 16 << 20
DIVERGE_BYTES = 16 << 20
CORRECT_BYTES = 24 << 20


def iota(shape, dim):
    return lax.broadcasted_iota(jnp.int32, shape, dim)


def halves(value):
    high = value.astype(BF16)
    return high, (value - high.astype(F32)).astype(BF16)


def dot(left, right):
    return jnp.dot(left, right, preferred_element_type=F32)


def dot_rows(left, right):
    return lax.dot_general(left, right, (((1,), (1,)), ((), ())), preferred_element_type=F32)


def hot(mask):
    return jnp.where(mask, 1.0, 0.0)


def pack_kernel(valid_counts, slab, row, fine, out, coarse, chosen, box, arrived, in_sems, out_sems):
    count_held = slab.shape[1]
    slab_count = chosen.shape[0] // SLOTS
    group = min(PACK_GROUP, slab_count)
    valid = valid_counts[0, 0]
    lane_base = lax.axis_index("slab") % 4 * SLOTS
    loads = [
        pltpu.make_async_copy(fine.at[part], arrived.at[part], in_sems.at[part]) for part in range(3)
    ]
    for load in loads:
        load.start()
    piece = min(LANES, count_held)
    before = hot(iota((piece, piece), 0) < iota((piece, piece), 1)).astype(BF16)
    pieces = range(0, count_held, piece)
    named_all, earlier_all, rank_all, running = [], [], [], jnp.zeros((slab_count, 1), F32)
    for start in pieces:
        live = iota((1, piece), 1) + start < valid
        target = jnp.where(live, slab[:, start : start + piece], -1)
        named = hot(iota((slab_count, piece), 0) == target)
        named_all.append(named)
    for named in named_all:
        earlier_all.append(dot(named.astype(BF16), before) + running)
        running = running + jnp.sum(named, axis=1, keepdims=True)
    table = jnp.zeros((slab_count, LANES), F32)
    for start, named, earlier in zip(pieces, named_all, earlier_all):
        lanes = slice(start, start + piece)
        rank = jnp.sum(named * earlier, axis=0, keepdims=True).astype(jnp.int32)
        rank_all.append(hot(iota((SLOTS, piece), 0) == rank).astype(BF16))
        tag = row[:, lanes] + 1
        place = hot(iota((LANES, piece), 0) == rank + lane_base).astype(BF16)
        upper = (named * (tag // 64).astype(F32)).astype(BF16)
        lower = (named * (tag % 64).astype(F32)).astype(BF16)
        table = table + dot_rows(upper, place) * 64.0 + dot_rows(lower, place)
    rank16 = jnp.concatenate(rank_all, axis=1)
    named16 = jnp.concatenate([named.astype(BF16) for named in named_all], axis=1)
    loads[0].wait()
    for g in range(slab_count):
        chosen[g * SLOTS : (g + 1) * SLOTS, :] = rank16 * named16[g : g + 1, :]
        start = g * BOX_ROWS + TAG_ROW
        box[start : start + 1, :] = table[g : g + 1]
    pick = jnp.where(
        iota((2 * LANES, LANES), 0) // 2 == iota((2 * LANES, LANES), 1), 0.5, 0.0
    ).astype(BF16)
    chunk = min(256, count_held)
    stores = []
    for part in range(3):
        if part > 0:
            loads[part].wait()
        for start in range(0, count_held, chunk):
            rows = slice(start, start + chunk)
            high, low = halves(arrived[part, rows, :])
            mean_high, mean_low = halves(dot(high, pick) + dot(low, pick))
            coarse[part, rows, 0:LANES] = mean_high
            coarse[part, rows, LANES:] = mean_low
        for first in range(0, slab_count, group):
            both = dot(chosen[first * SLOTS : (first + group) * SLOTS, :], coarse[part])
            rows = both[:, :LANES] + both[:, LANES:]
            for g in range(group):
                start = (first + g) * BOX_ROWS + part * SLOTS
                box[start : start + SLOTS, :] = rows[g * SLOTS : (g + 1) * SLOTS]
            if part == 2:
                at = slice(first * BOX_ROWS, (first + group) * BOX_ROWS)
                index = first // group
                store = pltpu.make_async_copy(box.at[at], out.at[at], out_sems.at[index])
                store.start()
                stores.append(store)
    for store in stores:
        store.wait()


def pack(valid_counts, slab, row, fine, slab_count):
    count_held = slab.shape[1]
    vmem = pl.BlockSpec(memory_space=pltpu.VMEM)
    hbm = pl.BlockSpec(memory_space=pltpu.HBM)
    return pl.pallas_call(
        pack_kernel,
        in_specs=[pl.BlockSpec(memory_space=pltpu.SMEM), vmem, vmem, hbm],
        out_specs=hbm,
        out_shape=jax.ShapeDtypeStruct((slab_count * BOX_ROWS, LANES), F32),
        scratch_shapes=[
            pltpu.VMEM((3, count_held, 2 * LANES), BF16),
            pltpu.VMEM((slab_count * SLOTS, count_held), BF16),
            pltpu.VMEM((slab_count * BOX_ROWS, LANES), F32),
            pltpu.VMEM((3, count_held, 2 * LANES), F32),
            pltpu.SemaphoreType.DMA((3,)),
            pltpu.SemaphoreType.DMA((max(1, slab_count // PACK_GROUP),)),
        ],
        compiler_params=pltpu.CompilerParams(vmem_limit_bytes=PACK_BYTES),
        name="pack",
    )(valid_counts, slab, row, fine)


OUTER, INNER = (0, 1, 6, 7), (2, 3, 4, 5)


def rows_of(tiles, tile):
    return slice(tiles.index(tile) * 8, tiles.index(tile) * 8 + 8)


def tile_of(outer, inner, part, z, tile):
    if tile in OUTER:
        return outer[part, z, rows_of(OUTER, tile), :]
    return inner[part, z, rows_of(INNER, tile), :]


def divergence_tile(outer, inner, z, tile):
    depth_z, width_x = outer.shape[1], outer.shape[3]
    face_x, face_y, face_z = (tile_of(outer, inner, part, z, tile) for part in range(3))
    above_z = tile_of(outer, inner, 2, z + 1, tile) if z + 1 < depth_z else 0.0
    next_x = jnp.where(
        iota((8, width_x), 1) == width_x - 1, 0.0, pltpu.roll(face_x, width_x - 1, 1)
    )
    after = tile_of(outer, inner, 1, z, tile + 1)[0:1] if tile < 7 else 0.0
    next_y = jnp.where(iota((8, width_x), 0) == 7, after, pltpu.roll(face_y, 7, 0))
    return (next_x - face_x) + (next_y - face_y) + (above_z - face_z)


def put_plane(low_planes, high_planes, depth_z, z, tile, value):
    if z > depth_z - 4:
        start = (z - depth_z + 3) * 64 + tile * 8
        low_planes[start : start + 8, :] = value
    if z < 2:
        start = z * 64 + tile * 8
        high_planes[start : start + 8, :] = value


def sum_tiles(tiles, rows16, line_hot, tile_hot, number, base, field):
    depth_z, depth_y, width_x = base.shape[1:]
    for low_z in range(0, depth_z, 2):
        pairs = [(z, tile) for z in (low_z, low_z + 1) for tile in tiles]
        line16 = line_hot[...]
        chosen = jnp.concatenate(
            [
                line16 * tile_hot[z * 8 + tile : z * 8 + tile + 1, :]
                for z, tile in pairs
            ],
            axis=0,
        )
        both = dot(chosen, rows16[...])
        for at, (z, tile) in enumerate(pairs):
            found = number[z * 8 + tile]
            scale = 1.0 / jnp.maximum(found, 1.0)
            rows = slice(at * 64, at * 64 + 64)
            from_rows, to_rows = slice(tile * 8, tile * 8 + 8), rows_of(tiles, tile)
            for part in range(3):
                totals = both[rows, part * LANES : (part + 1) * LANES]
                totals = totals + both[rows, (3 + part) * LANES : (4 + part) * LANES]
                averaged = totals * scale
                for xb in range(width_x // LANES):
                    xs, at8 = slice(xb * LANES, (xb + 1) * LANES), slice(xb * 8, xb * 8 + 8)
                    field[part, z, to_rows, xs] = jnp.where(
                        found[at8] > 0.5, averaged[at8], base[part, z, from_rows, xs]
                    )


def outer_kernel(
    box, base, field, low_rows, high_rows, rows16, line_hot, tile_hot, number
):
    slab_count = box.shape[0] // BOX_ROWS
    depth_z = base.shape[1]
    width = 3 * LANES
    tag_rows = [box[i * BOX_ROWS + TAG_ROW : (i + 1) * BOX_ROWS, :] for i in range(slab_count)]
    sums = [sum(tag_rows[i + 1 : i + 4], tag_rows[i]) for i in range(0, slab_count, 4)]
    tags = jnp.concatenate(sums, axis=0).astype(jnp.int32) - 1
    tiles, within = tags >> 6, tags & 63
    order = iota((64, LANES), 0)
    order = order % 8 * 8 + order // 8
    counts = jnp.zeros((64, tile_hot.shape[0]), F32)
    for g in range(slab_count // 4):
        lanes = slice(g * LANES, (g + 1) * LANES)
        line16 = hot(within[g : g + 1, :] == order).astype(BF16)
        tile16 = hot(tiles[g : g + 1, :] == iota((tile_hot.shape[0], LANES), 0)).astype(BF16)
        line_hot[:, lanes] = line16
        tile_hot[:, lanes] = tile16
        counts = counts + dot_rows(line16, tile16)
    for tile in range(tile_hot.shape[0]):
        number[tile] = jnp.broadcast_to(counts[:, tile : tile + 1], (64, LANES))
    for part in range(3):
        for i in range(slab_count):
            start = i * BOX_ROWS + part * SLOTS
            high, low = halves(box[start : start + SLOTS, :])
            rows = slice(i * SLOTS, (i + 1) * SLOTS)
            rows16[rows, part * LANES : (part + 1) * LANES] = high
            rows16[rows, width + part * LANES : width + (part + 1) * LANES] = low
    sum_tiles(OUTER, rows16, line_hot, tile_hot, number, base, field)
    for z in range(depth_z):
        high_rows[3 * z : 3 * z + 2, :] = divergence_tile(field, None, z, 0)[0:2]
        high_rows[3 * z + 2 : 3 * z + 3, :] = tile_of(field, None, 1, z, 0)[0:1]
        low_rows[3 * z : 3 * z + 3, :] = divergence_tile(field, None, z, 7)[5:8]
    end = 3 * depth_z
    low_rows[end : end + 3, :] = tile_of(field, None, 2, 0, 7)[5:8]
    high_rows[end : end + 3, :] = tile_of(field, None, 2, 0, 0)[0:3]


def inner_kernel(rows16, line_hot, tile_hot, number, base, field):
    sum_tiles(INNER, rows16, line_hot, tile_hot, number, base, field)


def vmem_call(kernel, shapes, limit, name):
    vmem = pl.BlockSpec(memory_space=pltpu.VMEM)
    return lambda *operands: pl.pallas_call(
        kernel,
        in_specs=[vmem] * len(operands),
        out_specs=[vmem] * len(shapes),
        out_shape=[jax.ShapeDtypeStruct(dims, dtype) for dims, dtype in shapes],
        compiler_params=pltpu.CompilerParams(vmem_limit_bytes=limit),
        name=name,
    )(*operands)


def sum_outer(box, base):
    slots = box.shape[0] // BOX_ROWS * SLOTS
    _, depth_z, depth_y, width_x = base.shape
    line_count = -(-3 * (depth_z + 1) // 8) * 8
    shapes = [
        ((3, depth_z, 8 * len(OUTER), width_x), F32),
        ((line_count, width_x), F32),
        ((line_count, width_x), F32),
        ((slots, 6 * LANES), BF16),
        ((64, slots), BF16),
        ((depth_z * depth_y // 8, slots), BF16),
        ((depth_z * depth_y // 8, 64, LANES), F32),
    ]
    return vmem_call(outer_kernel, shapes, OUTER_BYTES, "sum_outer")(box, base)


def sum_inner(tables, base):
    _, depth_z, _, width_x = base.shape
    shapes = [((3, depth_z, 8 * len(INNER), width_x), F32)]
    return vmem_call(inner_kernel, shapes, INNER_BYTES, "sum_inner")(*tables, base)[0]


def diverge_kernel(outer, inner, own, below, above, partial, beside, low_planes, high_planes):
    depth_z = outer.shape[1]
    for z in range(depth_z):
        for tile in range(8):
            value = divergence_tile(outer, inner, z, tile)
            if tile == 7:
                face = above[3 * z + 2 : 3 * z + 3, :]
                value = value + jnp.where(iota(value.shape, 0) == 7, face, 0.0)
            rows = slice(tile * 8, tile * 8 + 8)
            partial[z, rows, :] = value
            put_plane(low_planes, high_planes, depth_z, z, tile, value)
            if z == 0:
                high_planes[128 + tile * 8 : 136 + tile * 8, :] = tile_of(outer, inner, 2, 0, tile)
    for z in range(depth_z + 1):
        beside[z, 0:3, :] = above[3 * z : 3 * z + 3, :]
        beside[z, 3:5, :] = jnp.zeros_like(beside[z, 3:5, :])
        under = below[3 * z : 3 * z + 3, :]
        if z < depth_z:
            face = own[3 * z + 2 : 3 * z + 3, :]
            under = under + jnp.where(iota(under.shape, 0) == 2, face, 0.0)
        beside[z, 5:8, :] = under
    low_planes[192:200, :] = beside[depth_z - 1]
    low_planes[194:195, :] = beside[depth_z - 2, 0:1, :]
    low_planes[197:198, :] = beside[depth_z - 2, 7:8, :]
    high_planes[192:200, :] = beside[0]
    high_planes[197:198, :] = beside[1, 7:8, :]
    high_planes[200:208, :] = beside[depth_z]


def diverge(outer, inner, own, below, above):
    depth_z, width_x = outer.shape[1], outer.shape[3]
    shapes = [((depth_z, 64, width_x), F32), ((depth_z + 1, 8, width_x), F32)]
    shapes += [((200, width_x), F32), ((208, width_x), F32)]
    return vmem_call(diverge_kernel, shapes, DIVERGE_BYTES, "diverge")(
        outer, inner, own, below, above
    )


def correct_kernel(
    outer, inner, partial, beside, below, above, active,
    out, first, second, third, active_here, out_here, in_sem, out_sems
):
    depth_z, depth_y, width_x = partial.shape
    planes = depth_z + 5
    tiles = depth_y // 8 + 2
    line = iota((8, width_x), 0)
    column = iota((8, width_x), 1)
    slab_at, band_at = lax.axis_index("slab"), lax.axis_index("pencil")
    has_low_z = jnp.where(slab_at > 0, 1.0, 0.0)
    has_high_z = jnp.where(slab_at < lax.axis_size("slab") - 1, 1.0, 0.0)
    has_low_y = jnp.where(band_at > 0, 1.0, 0.0)
    has_high_y = jnp.where(band_at < lax.axis_size("pencil") - 1, 1.0, 0.0)
    load = pltpu.make_async_copy(active, active_here, in_sem)
    load.start()
    sixth = 1.0 / 6.0

    def z_scale(p):
        return has_low_z if p < 3 else (has_high_z if p >= depth_z + 3 else 1.0)

    def y_scale(t):
        return has_low_y if t == 0 else (has_high_y if t == tiles - 1 else 1.0)

    def halo_tile(planes, plane, t, away):
        if 0 < t < tiles - 1:
            return planes[plane * 64 + t * 8 - 8 : plane * 64 + t * 8, :]
        if away > 1:
            return jnp.zeros((8, width_x), F32)
        value = planes[192:200, :]
        return value if away == 0 else pltpu.roll(value, 2 if t == 0 else 6, 0)

    def fill(p):
        z = p - 3
        for t in range(tiles):
            inside = 0 < t < tiles - 1
            rows = slice(t * 8 - 8, t * 8)
            if z < 0:
                value = halo_tile(below, p, t, 2 - p)
                if z == -1:
                    value = value + (tile_of(outer, inner, 2, 0, t - 1) if inside else beside[depth_z])
            elif z < depth_z:
                value = partial[z, rows, :] if inside else beside[z]
                if z == depth_z - 1:
                    value = value + (halo_tile(above, 2, t, 0) if inside else above[200:208, :])
            else:
                value = halo_tile(above, z - depth_z, t, z - depth_z)
            first[p, t * 8 : t * 8 + 8, :] = value * (-sixth * z_scale(p) * y_scale(t))

    def around(source, p, t):
        centre = source[p, t * 8 : t * 8 + 8, :]
        total = source[p - 1, t * 8 : t * 8 + 8, :] + source[p + 1, t * 8 : t * 8 + 8, :]
        lower = source[p, t * 8 - 1 : t * 8, :] if t > 0 else 0.0
        upper = source[p, t * 8 + 8 : t * 8 + 9, :] if t < tiles - 1 else 0.0
        total = total + jnp.where(line == 0, lower, pltpu.roll(centre, 1, 0))
        total = total + jnp.where(line == 7, upper, pltpu.roll(centre, 7, 0))
        total = total + jnp.where(column == 0, 0.0, pltpu.roll(centre, 1, 1))
        return total + jnp.where(column == width_x - 1, 0.0, pltpu.roll(centre, width_x - 1, 1))

    def sweep(source, target, p, count):
        for t in range(count):
            value = around(source, p, t) * sixth + first[p, t * 8 : t * 8 + 8, :]
            scaled = not (3 <= p < depth_z + 3 and 0 < t < tiles - 1)
            target[p, t * 8 : t * 8 + 8, :] = value * (z_scale(p) * y_scale(t)) if scaled else value

    def finish(z):
        p = z + 3
        for t in range(1, tiles - 1):
            ys, rows = slice(t * 8 - 8, t * 8), slice(t * 8, t * 8 + 8)
            mask = active_here[z, ys, :].astype(F32)
            centre = third[p, rows, :]
            left = jnp.where(column == 0, 0.0, pltpu.roll(centre, 1, 1))
            lower = jnp.where(line == 0, third[p, t * 8 - 1 : t * 8, :], pltpu.roll(centre, 1, 0))
            under = third[p - 1, rows, :]
            for part, other in enumerate((left, lower, under)):
                face = tile_of(outer, inner, part, z, t - 1)
                out_here[part, z, ys, :] = face - mask * (centre - other)
        store = pltpu.make_async_copy(out_here.at[:, z], out.at[:, z], out_sems.at[z])
        store.start()
        return store

    fill(0)
    fill(1)
    load.wait()
    stores = []
    for p in range(1, planes - 1):
        fill(p + 1)
        sweep(first, second, p, tiles)
        if p > 2:
            sweep(second, third, p - 1, tiles - 1)
        if p > 3:
            stores.append(finish(p - 4))
    for store in stores:
        store.wait()


def correct(outer, inner, partial, beside, below, above, active):
    depth_z, depth_y, width_x = partial.shape
    extended = pltpu.VMEM((depth_z + 5, depth_y + 16, width_x), F32)
    vmem = pl.BlockSpec(memory_space=pltpu.VMEM)
    hbm = pl.BlockSpec(memory_space=pltpu.HBM)
    out_dims = (3, depth_z, depth_y, width_x)
    return pl.pallas_call(
        correct_kernel,
        in_specs=[vmem] * 6 + [hbm],
        out_specs=hbm,
        out_shape=jax.ShapeDtypeStruct(out_dims, F32),
        scratch_shapes=[extended] * 3
        + [
            pltpu.VMEM(active.shape, active.dtype),
            pltpu.VMEM(out_dims, F32),
            pltpu.SemaphoreType.DMA,
            pltpu.SemaphoreType.DMA((depth_z,)),
        ],
        compiler_params=pltpu.CompilerParams(vmem_limit_bytes=CORRECT_BYTES),
        name="correct",
    )(outer, inner, partial, beside, below, above, active)


def moved(value, axis, steps):
    count = lax.axis_size(axis)
    pairs = [(i, i + steps) for i in range(count) if 0 <= i + steps < count]
    return lax.ppermute(value, axis, pairs)


def shards(fine_blocks, owner_slab, owner_row, valid_counts, coarse_field, active):
    slab_count = lax.axis_size("slab")
    count_held = fine_blocks.shape[1]
    fine = fine_blocks[0].transpose(1, 0, 2)
    out_box = pack(valid_counts, owner_slab.reshape(1, count_held), owner_row, fine, slab_count)
    out_box = out_box.reshape(slab_count, BOX_ROWS, 1, LANES)
    box = lax.all_to_all(out_box, "slab", split_axis=0, concat_axis=0, tiled=True)
    box = box.reshape(slab_count * BOX_ROWS, LANES)
    outer, low_rows, high_rows, *tables = sum_outer(box, coarse_field)
    rows_below = moved(low_rows, "pencil", 1)
    rows_above = moved(high_rows, "pencil", -1)
    inner = sum_inner(tables, coarse_field)
    partial, beside, low_planes, high_planes = diverge(
        outer, inner, high_rows, rows_below, rows_above
    )
    below = moved(low_planes, "slab", 1)
    above = moved(high_planes, "slab", -1)
    return correct(outer, inner, partial, beside, below, above, active)


def solution(mesh):
    in_specs = (
        P("pencil", "slab", None, None),
        P("pencil", "slab", None),
        P("pencil", "slab"),
        P("pencil", "slab"),
        P(None, "slab", "pencil", None),
        P("slab", "pencil", None),
    )
    out_specs = P(None, "slab", "pencil", None)
    return jax.shard_map(shards, mesh=mesh, in_specs=in_specs, out_specs=out_specs, check_vma=False)
```

```python
import jax
import jax.numpy as jnp
from jax import lax
from jax.experimental import pallas as pl
from jax.experimental.pallas import tpu as pltpu
from jax.sharding import PartitionSpec as P

F32, BF16 = jnp.float32, jnp.bfloat16
LANES = 128
SLOTS = 32
TAG_ROW = 3 * SLOTS
BOX_ROWS = TAG_ROW + 1
PACK_GROUP = 16
PACK_BYTES = 60 << 20
OUTER_BYTES = 24 << 20
INNER_BYTES = 16 << 20
DIVERGE_BYTES = 16 << 20
CORRECT_BYTES = 24 << 20


def iota(shape, dim):
    return lax.broadcasted_iota(jnp.int32, shape, dim)


def halves(value):
    high = value.astype(BF16)
    return high, (value - high.astype(F32)).astype(BF16)


def dot(left, right):
    return jnp.dot(left, right, preferred_element_type=F32)


def dot_rows(left, right):
    return lax.dot_general(left, right, (((1,), (1,)), ((), ())), preferred_element_type=F32)


def hot(mask):
    return jnp.where(mask, 1.0, 0.0)


def pack_kernel(valid_counts, slab, row, fine, out, coarse, chosen, box, arrived, in_sems, out_sems):
    count_held = slab.shape[1]
    slab_count = chosen.shape[0] // SLOTS
    group = min(PACK_GROUP, slab_count)
    valid = valid_counts[0, 0]
    lane_base = lax.axis_index("slab") % 4 * SLOTS
    loads = [
        pltpu.make_async_copy(fine.at[part], arrived.at[part], in_sems.at[part]) for part in range(3)
    ]
    for load in loads:
        load.start()
    piece = min(LANES, count_held)
    before = hot(iota((piece, piece), 0) < iota((piece, piece), 1)).astype(BF16)
    pieces = range(0, count_held, piece)
    named_all, earlier_all, rank_all, running = [], [], [], jnp.zeros((slab_count, 1), F32)
    for start in pieces:
        live = iota((1, piece), 1) + start < valid
        target = jnp.where(live, slab[:, start : start + piece], -1)
        named = hot(iota((slab_count, piece), 0) == target)
        named_all.append(named)
    for named in named_all:
        earlier_all.append(dot(named.astype(BF16), before) + running)
        running = running + jnp.sum(named, axis=1, keepdims=True)
    table = jnp.zeros((slab_count, LANES), F32)
    for start, named, earlier in zip(pieces, named_all, earlier_all):
        lanes = slice(start, start + piece)
        rank = jnp.sum(named * earlier, axis=0, keepdims=True).astype(jnp.int32)
        rank_all.append(hot(iota((SLOTS, piece), 0) == rank).astype(BF16))
        tag = row[:, lanes] + 1
        place = hot(iota((LANES, piece), 0) == rank + lane_base).astype(BF16)
        upper = (named * (tag // 64).astype(F32)).astype(BF16)
        lower = (named * (tag % 64).astype(F32)).astype(BF16)
        table = table + dot_rows(upper, place) * 64.0 + dot_rows(lower, place)
    rank16 = jnp.concatenate(rank_all, axis=1)
    named16 = jnp.concatenate([named.astype(BF16) for named in named_all], axis=1)
    loads[0].wait()
    for g in range(slab_count):
        chosen[g * SLOTS : (g + 1) * SLOTS, :] = rank16 * named16[g : g + 1, :]
        start = g * BOX_ROWS + TAG_ROW
        box[start : start + 1, :] = table[g : g + 1]
    pick = jnp.where(
        iota((2 * LANES, LANES), 0) // 2 == iota((2 * LANES, LANES), 1), 0.5, 0.0
    ).astype(BF16)
    chunk = min(256, count_held)
    stores = []
    for part in range(3):
        if part > 0:
            loads[part].wait()
        for start in range(0, count_held, chunk):
            rows = slice(start, start + chunk)
            high, low = halves(arrived[part, rows, :])
            mean_high, mean_low = halves(dot(high, pick) + dot(low, pick))
            coarse[part, rows, 0:LANES] = mean_high
            coarse[part, rows, LANES:] = mean_low
        for first in range(0, slab_count, group):
            both = dot(chosen[first * SLOTS : (first + group) * SLOTS, :], coarse[part])
            rows = both[:, :LANES] + both[:, LANES:]
            for g in range(group):
                start = (first + g) * BOX_ROWS + part * SLOTS
                box[start : start + SLOTS, :] = rows[g * SLOTS : (g + 1) * SLOTS]
            if part == 2:
                at = slice(first * BOX_ROWS, (first + group) * BOX_ROWS)
                index = first // group
                store = pltpu.make_async_copy(box.at[at], out.at[at], out_sems.at[index])
                store.start()
                stores.append(store)
    for store in stores:
        store.wait()


def pack(valid_counts, slab, row, fine, slab_count):
    count_held = slab.shape[1]
    vmem = pl.BlockSpec(memory_space=pltpu.VMEM)
    hbm = pl.BlockSpec(memory_space=pltpu.HBM)
    return pl.pallas_call(
        pack_kernel,
        in_specs=[pl.BlockSpec(memory_space=pltpu.SMEM), vmem, vmem, hbm],
        out_specs=hbm,
        out_shape=jax.ShapeDtypeStruct((slab_count * BOX_ROWS, LANES), F32),
        scratch_shapes=[
            pltpu.VMEM((3, count_held, 2 * LANES), BF16),
            pltpu.VMEM((slab_count * SLOTS, count_held), BF16),
            pltpu.VMEM((slab_count * BOX_ROWS, LANES), F32),
            pltpu.VMEM((3, count_held, 2 * LANES), F32),
            pltpu.SemaphoreType.DMA((3,)),
            pltpu.SemaphoreType.DMA((max(1, slab_count // PACK_GROUP),)),
        ],
        compiler_params=pltpu.CompilerParams(vmem_limit_bytes=PACK_BYTES),
        name="pack",
    )(valid_counts, slab, row, fine)


OUTER, INNER = (0, 1, 6, 7), (2, 3, 4, 5)


def rows_of(tiles, tile):
    return slice(tiles.index(tile) * 8, tiles.index(tile) * 8 + 8)


def tile_of(outer, inner, part, z, tile):
    if tile in OUTER:
        return outer[part, z, rows_of(OUTER, tile), :]
    return inner[part, z, rows_of(INNER, tile), :]


def divergence_tile(outer, inner, z, tile):
    depth_z, width_x = outer.shape[1], outer.shape[3]
    face_x, face_y, face_z = (tile_of(outer, inner, part, z, tile) for part in range(3))
    above_z = tile_of(outer, inner, 2, z + 1, tile) if z + 1 < depth_z else 0.0
    next_x = jnp.where(
        iota((8, width_x), 1) == width_x - 1, 0.0, pltpu.roll(face_x, width_x - 1, 1)
    )
    after = tile_of(outer, inner, 1, z, tile + 1)[0:1] if tile < 7 else 0.0
    next_y = jnp.where(iota((8, width_x), 0) == 7, after, pltpu.roll(face_y, 7, 0))
    return (next_x - face_x) + (next_y - face_y) + (above_z - face_z)


def put_plane(low_planes, high_planes, depth_z, z, tile, value):
    if z > depth_z - 4:
        start = (z - depth_z + 3) * 64 + tile * 8
        low_planes[start : start + 8, :] = value
    if z < 2:
        start = z * 64 + tile * 8
        high_planes[start : start + 8, :] = value


def sum_tiles(tiles, rows16, line_hot, tile_hot, number, base, field):
    depth_z, depth_y, width_x = base.shape[1:]
    for low_z in range(0, depth_z, 2):
        pairs = [(z, tile) for z in (low_z, low_z + 1) for tile in tiles]
        line16 = line_hot[...]
        chosen = jnp.concatenate(
            [
                line16 * tile_hot[z * 8 + tile : z * 8 + tile + 1, :]
                for z, tile in pairs
            ],
            axis=0,
        )
        both = dot(chosen, rows16[...])
        for at, (z, tile) in enumerate(pairs):
            found = number[z * 8 + tile]
            scale = 1.0 / jnp.maximum(found, 1.0)
            rows = slice(at * 64, at * 64 + 64)
            from_rows, to_rows = slice(tile * 8, tile * 8 + 8), rows_of(tiles, tile)
            for part in range(3):
                totals = both[rows, part * LANES : (part + 1) * LANES]
                totals = totals + both[rows, (3 + part) * LANES : (4 + part) * LANES]
                averaged = totals * scale
                for xb in range(width_x // LANES):
                    xs, at8 = slice(xb * LANES, (xb + 1) * LANES), slice(xb * 8, xb * 8 + 8)
                    field[part, z, to_rows, xs] = jnp.where(
                        found[at8] > 0.5, averaged[at8], base[part, z, from_rows, xs]
                    )


def outer_kernel(
    box, base, field, low_rows, high_rows, rows16, line_hot, tile_hot, number
):
    slab_count = box.shape[0] // BOX_ROWS
    depth_z = base.shape[1]
    width = 3 * LANES
    tag_rows = [box[i * BOX_ROWS + TAG_ROW : (i + 1) * BOX_ROWS, :] for i in range(slab_count)]
    sums = [sum(tag_rows[i + 1 : i + 4], tag_rows[i]) for i in range(0, slab_count, 4)]
    tags = jnp.concatenate(sums, axis=0).astype(jnp.int32) - 1
    tiles, within = tags >> 6, tags & 63
    order = iota((64, LANES), 0)
    order = order % 8 * 8 + order // 8
    counts = jnp.zeros((64, tile_hot.shape[0]), F32)
    for g in range(slab_count // 4):
        lanes = slice(g * LANES, (g + 1) * LANES)
        line16 = hot(within[g : g + 1, :] == order).astype(BF16)
        tile16 = hot(tiles[g : g + 1, :] == iota((tile_hot.shape[0], LANES), 0)).astype(BF16)
        line_hot[:, lanes] = line16
        tile_hot[:, lanes] = tile16
        counts = counts + dot_rows(line16, tile16)
    for tile in range(tile_hot.shape[0]):
        number[tile] = jnp.broadcast_to(counts[:, tile : tile + 1], (64, LANES))
    for part in range(3):
        for i in range(slab_count):
            start = i * BOX_ROWS + part * SLOTS
            high, low = halves(box[start : start + SLOTS, :])
            rows = slice(i * SLOTS, (i + 1) * SLOTS)
            rows16[rows, part * LANES : (part + 1) * LANES] = high
            rows16[rows, width + part * LANES : width + (part + 1) * LANES] = low
    sum_tiles(OUTER, rows16, line_hot, tile_hot, number, base, field)
    for z in range(depth_z):
        high_rows[3 * z : 3 * z + 2, :] = divergence_tile(field, None, z, 0)[0:2]
        high_rows[3 * z + 2 : 3 * z + 3, :] = tile_of(field, None, 1, z, 0)[0:1]
        low_rows[3 * z : 3 * z + 3, :] = divergence_tile(field, None, z, 7)[5:8]
    end = 3 * depth_z
    low_rows[end : end + 3, :] = tile_of(field, None, 2, 0, 7)[5:8]
    high_rows[end : end + 3, :] = tile_of(field, None, 2, 0, 0)[0:3]


def inner_kernel(rows16, line_hot, tile_hot, number, base, field):
    sum_tiles(INNER, rows16, line_hot, tile_hot, number, base, field)


def vmem_call(kernel, shapes, limit, name):
    vmem = pl.BlockSpec(memory_space=pltpu.VMEM)
    return lambda *operands: pl.pallas_call(
        kernel,
        in_specs=[vmem] * len(operands),
        out_specs=[vmem] * len(shapes),
        out_shape=[jax.ShapeDtypeStruct(dims, dtype) for dims, dtype in shapes],
        compiler_params=pltpu.CompilerParams(vmem_limit_bytes=limit),
        name=name,
    )(*operands)


def sum_outer(box, base):
    slots = box.shape[0] // BOX_ROWS * SLOTS
    _, depth_z, depth_y, width_x = base.shape
    line_count = -(-3 * (depth_z + 1) // 8) * 8
    shapes = [
        ((3, depth_z, 8 * len(OUTER), width_x), F32),
        ((line_count, width_x), F32),
        ((line_count, width_x), F32),
        ((slots, 6 * LANES), BF16),
        ((64, slots), BF16),
        ((depth_z * depth_y // 8, slots), BF16),
        ((depth_z * depth_y // 8, 64, LANES), F32),
    ]
    return vmem_call(outer_kernel, shapes, OUTER_BYTES, "sum_outer")(box, base)


def sum_inner(tables, base):
    _, depth_z, _, width_x = base.shape
    shapes = [((3, depth_z, 8 * len(INNER), width_x), F32)]
    return vmem_call(inner_kernel, shapes, INNER_BYTES, "sum_inner")(*tables, base)[0]


def diverge_kernel(outer, inner, own, below, above, partial, beside, low_planes, high_planes):
    depth_z = outer.shape[1]
    for z in range(depth_z):
        for tile in range(8):
            value = divergence_tile(outer, inner, z, tile)
            if tile == 7:
                face = above[3 * z + 2 : 3 * z + 3, :]
                value = value + jnp.where(iota(value.shape, 0) == 7, face, 0.0)
            rows = slice(tile * 8, tile * 8 + 8)
            partial[z, rows, :] = value
            put_plane(low_planes, high_planes, depth_z, z, tile, value)
            if z == 0:
                high_planes[128 + tile * 8 : 136 + tile * 8, :] = tile_of(outer, inner, 2, 0, tile)
    for z in range(depth_z + 1):
        beside[z, 0:3, :] = above[3 * z : 3 * z + 3, :]
        beside[z, 3:5, :] = jnp.zeros_like(beside[z, 3:5, :])
        under = below[3 * z : 3 * z + 3, :]
        if z < depth_z:
            face = own[3 * z + 2 : 3 * z + 3, :]
            under = under + jnp.where(iota(under.shape, 0) == 2, face, 0.0)
        beside[z, 5:8, :] = under
    low_planes[192:200, :] = beside[depth_z - 1]
    low_planes[200:208, :] = jnp.zeros_like(low_planes[200:208, :])
    low_planes[194:195, :] = beside[depth_z - 2, 0:1, :]
    low_planes[197:198, :] = beside[depth_z - 2, 7:8, :]
    high_planes[192:200, :] = beside[0]
    high_planes[197:198, :] = beside[1, 7:8, :]
    high_planes[200:208, :] = beside[depth_z]


def diverge(outer, inner, own, below, above):
    depth_z, width_x = outer.shape[1], outer.shape[3]
    shapes = [((depth_z, 64, width_x), F32), ((depth_z + 1, 8, width_x), F32)]
    shapes += [((208, width_x), F32)] * 2
    return vmem_call(diverge_kernel, shapes, DIVERGE_BYTES, "diverge")(
        outer, inner, own, below, above
    )


def correct_kernel(
    outer, inner, partial, beside, below, above, active,
    out, first, second, third, active_here, out_here, in_sem, out_sems
):
    depth_z, depth_y, width_x = partial.shape
    planes = depth_z + 5
    tiles = depth_y // 8 + 2
    line = iota((8, width_x), 0)
    column = iota((8, width_x), 1)
    slab_at, band_at = lax.axis_index("slab"), lax.axis_index("pencil")
    has_low_z = jnp.where(slab_at > 0, 1.0, 0.0)
    has_high_z = jnp.where(slab_at < lax.axis_size("slab") - 1, 1.0, 0.0)
    has_low_y = jnp.where(band_at > 0, 1.0, 0.0)
    has_high_y = jnp.where(band_at < lax.axis_size("pencil") - 1, 1.0, 0.0)
    load = pltpu.make_async_copy(active, active_here, in_sem)
    load.start()
    sixth = 1.0 / 6.0

    def z_scale(p):
        return has_low_z if p < 3 else (has_high_z if p >= depth_z + 3 else 1.0)

    def y_scale(t):
        return has_low_y if t == 0 else (has_high_y if t == tiles - 1 else 1.0)

    def halo_tile(planes, plane, t, away):
        if 0 < t < tiles - 1:
            return planes[plane * 64 + t * 8 - 8 : plane * 64 + t * 8, :]
        if away > 1:
            return jnp.zeros((8, width_x), F32)
        value = planes[192:200, :]
        return value if away == 0 else pltpu.roll(value, 2 if t == 0 else 6, 0)

    def fill(p):
        z = p - 3
        for t in range(tiles):
            inside = 0 < t < tiles - 1
            rows = slice(t * 8 - 8, t * 8)
            if z < 0:
                value = halo_tile(below, p, t, 2 - p)
                if z == -1:
                    value = value + (tile_of(outer, inner, 2, 0, t - 1) if inside else beside[depth_z])
            elif z < depth_z:
                value = partial[z, rows, :] if inside else beside[z]
                if z == depth_z - 1:
                    value = value + (halo_tile(above, 2, t, 0) if inside else above[200:208, :])
            else:
                value = halo_tile(above, z - depth_z, t, z - depth_z)
            first[p, t * 8 : t * 8 + 8, :] = value * (-sixth * z_scale(p) * y_scale(t))

    def around(source, p, t):
        centre = source[p, t * 8 : t * 8 + 8, :]
        total = source[p - 1, t * 8 : t * 8 + 8, :] + source[p + 1, t * 8 : t * 8 + 8, :]
        lower = source[p, t * 8 - 1 : t * 8, :] if t > 0 else 0.0
        upper = source[p, t * 8 + 8 : t * 8 + 9, :] if t < tiles - 1 else 0.0
        total = total + jnp.where(line == 0, lower, pltpu.roll(centre, 1, 0))
        total = total + jnp.where(line == 7, upper, pltpu.roll(centre, 7, 0))
        total = total + jnp.where(column == 0, 0.0, pltpu.roll(centre, 1, 1))
        return total + jnp.where(column == width_x - 1, 0.0, pltpu.roll(centre, width_x - 1, 1))

    def sweep(source, target, p, count):
        for t in range(count):
            value = around(source, p, t) * sixth + first[p, t * 8 : t * 8 + 8, :]
            scaled = not (3 <= p < depth_z + 3 and 0 < t < tiles - 1)
            target[p, t * 8 : t * 8 + 8, :] = value * (z_scale(p) * y_scale(t)) if scaled else value

    def finish(z):
        p = z + 3
        for t in range(1, tiles - 1):
            ys, rows = slice(t * 8 - 8, t * 8), slice(t * 8, t * 8 + 8)
            mask = active_here[z, ys, :].astype(F32)
            centre = third[p, rows, :]
            left = jnp.where(column == 0, 0.0, pltpu.roll(centre, 1, 1))
            lower = jnp.where(line == 0, third[p, t * 8 - 1 : t * 8, :], pltpu.roll(centre, 1, 0))
            under = third[p - 1, rows, :]
            for part, other in enumerate((left, lower, under)):
                face = tile_of(outer, inner, part, z, t - 1)
                out_here[part, z, ys, :] = face - mask * (centre - other)
        store = pltpu.make_async_copy(out_here.at[:, z], out.at[:, z], out_sems.at[z])
        store.start()
        return store

    fill(0)
    fill(1)
    load.wait()
    stores = []
    for p in range(1, planes - 1):
        fill(p + 1)
        sweep(first, second, p, tiles)
        if p > 2:
            sweep(second, third, p - 1, tiles - 1)
        if p > 3:
            stores.append(finish(p - 4))
    for store in stores:
        store.wait()


def correct(outer, inner, partial, beside, below, above, active):
    depth_z, depth_y, width_x = partial.shape
    extended = pltpu.VMEM((depth_z + 5, depth_y + 16, width_x), F32)
    vmem = pl.BlockSpec(memory_space=pltpu.VMEM)
    hbm = pl.BlockSpec(memory_space=pltpu.HBM)
    out_dims = (3, depth_z, depth_y, width_x)
    return pl.pallas_call(
        correct_kernel,
        in_specs=[vmem] * 6 + [hbm],
        out_specs=hbm,
        out_shape=jax.ShapeDtypeStruct(out_dims, F32),
        scratch_shapes=[extended] * 3
        + [
            pltpu.VMEM(active.shape, active.dtype),
            pltpu.VMEM(out_dims, F32),
            pltpu.SemaphoreType.DMA,
            pltpu.SemaphoreType.DMA((depth_z,)),
        ],
        compiler_params=pltpu.CompilerParams(vmem_limit_bytes=CORRECT_BYTES),
        name="correct",
    )(outer, inner, partial, beside, below, above, active)


def moved(value, axis, steps):
    count = lax.axis_size(axis)
    pairs = [(i, i + steps) for i in range(count) if 0 <= i + steps < count]
    return lax.ppermute(value, axis, pairs)


def shards(fine_blocks, owner_slab, owner_row, valid_counts, coarse_field, active):
    slab_count = lax.axis_size("slab")
    count_held = fine_blocks.shape[1]
    fine = fine_blocks[0].transpose(1, 0, 2)
    out_box = pack(valid_counts, owner_slab.reshape(1, count_held), owner_row, fine, slab_count)
    out_box = out_box.reshape(slab_count, BOX_ROWS, 1, LANES)
    box = lax.all_to_all(out_box, "slab", split_axis=0, concat_axis=0, tiled=True)
    box = box.reshape(slab_count * BOX_ROWS, LANES)
    outer, low_rows, high_rows, *tables = sum_outer(box, coarse_field)
    rows_below = moved(low_rows, "pencil", 1)
    rows_above = moved(high_rows, "pencil", -1)
    inner = sum_inner(tables, coarse_field)
    partial, beside, low_planes, high_planes = diverge(
        outer, inner, high_rows, rows_below, rows_above
    )
    below = moved(low_planes, "slab", 1)
    above = moved(high_planes, "slab", -1)
    return correct(outer, inner, partial, beside, below, above, active)


def solution(mesh):
    in_specs = (
        P("pencil", "slab", None, None),
        P("pencil", "slab", None),
        P("pencil", "slab"),
        P("pencil", "slab"),
        P(None, "slab", "pencil", None),
        P("slab", "pencil", None),
    )
    out_specs = P(None, "slab", "pencil", None)
    return jax.shard_map(shards, mesh=mesh, in_specs=in_specs, out_specs=out_specs, check_vma=False)
```
